32 devices in a mesh: parts: 2 (over y), node: 4 (over x, core), tm: 4 (over z).
Axes of the slice: x: 2, y: 2, z: 4, core: 2. Of those that a mesh axis runs over, the one named last changes fastest.
Arguments:
- field: bfloat16 [12288, 2048], P(('parts', 'node', 'tm')), parts along dimension 0, may hold values from -6 to 6
- node_geometry: float32 [4, 6144], P(None, ('node', 'tm')), may hold values from 0 to 3, as said below
- taps: bfloat16 [65], replicated, may hold values from 0.049804688 to 0.19921875
- boundary: int32 [4, 8], P('node'), may hold values from 0 to 11, as said below
- sends: int32 [4, 4, 4], replicated, may hold values from 0 to 7, as said below
- cols: int32 [48, 16], P('node'), may hold values from 0 to 27, as said below
Outputs:
- applied: bfloat16 [12288, 2048], P(('parts', 'node'), 'tm'), parts along dimension 0
The draws below stay inside these ranges and needn't reach their ends.
There are 2 independent parts, one for each index of `parts`. The reference program is written for one: setup_inputs(seed, part) draws one part's arguments, and reference() takes and returns one part's arrays. A program takes and returns all parts, laid end to end along the dimension named above; an argument that names none is the same for every part. Nothing has to cross between parts.
Inputs may be any that keep to these rules, and one draw needn't show every extreme that they name: Each row of boundary holds distinct partition-local block numbers. sends[p, q] holds distinct positions of p's boundary list. `cols`: the first 12 entries of a row block's list are below 12, the first being the row block's own partition-local number; the others name slots of partitions other than the row block's own. `node_geometry`: coordinates lie in [0, 1], amplitudes in [0.3, 3].
All inputs are finite; a program needn't handle non-finite values.
Results may differ from the reference program's by a relative error of at most 0.0057.
Values may be sent and summed in bfloat16 or wider, within the bound.
A program may use at most 64 MiB of HBM per device.

```python
import math
import jax
import jax.numpy as jnp
from jax import lax

BLK = 128
STEPS = 2048
BAND = 32
NNZ = 16
NREM = 4
BOUNDARY_BLOCKS = 8
SEND = 4
PARTITION_COUNT = 4
PB = 12
NBLK = 48
NODES = 6144


def pattern(key):
    bkey = jax.random.fold_in(key, 101)
    sample_key = jax.random.fold_in(key, 102)
    ckey = jax.random.fold_in(key, 103)
    lkey = jax.random.fold_in(key, 104)
    okey = jax.random.fold_in(key, 105)
    qkey = jax.random.fold_in(key, 106)
    bscore = jax.random.randint(bkey, (PARTITION_COUNT, PB), 0, 1 << 20) * PB + jnp.arange(PB)[None, :]
    bscore = bscore.at[0, PB - 1].set(-1)
    boundary = jnp.argsort(bscore, axis=1)[:, :BOUNDARY_BLOCKS].astype(jnp.int32)
    sender_rank_score = jax.random.randint(sample_key, (PARTITION_COUNT, PARTITION_COUNT, BOUNDARY_BLOCKS), 0, 1 << 20) * BOUNDARY_BLOCKS + jnp.arange(BOUNDARY_BLOCKS)[None, None, :]
    sender_rank_score = sender_rank_score.at[0, :, BOUNDARY_BLOCKS - 1].set(-1)
    sends = jnp.argsort(sender_rank_score, axis=2)[:, :, :SEND].astype(jnp.int32)
    counts = jax.random.randint(ckey, (PARTITION_COUNT, PARTITION_COUNT), 1, SEND + 1)
    cycle = (jnp.arange(PARTITION_COUNT)[:, None] + 1) % PARTITION_COUNT == jnp.arange(PARTITION_COUNT)[None, :]
    counts = jnp.where(cycle, SEND, counts)
    rows = jnp.arange(NBLK)
    home = rows // PB
    local = jax.random.randint(lkey, (NBLK, NNZ - NREM), 0, PB)
    local = local.at[:, 0].set(rows % PB)
    offset = jax.random.randint(okey, (NBLK, NREM), 1, PARTITION_COUNT)
    first = (rows % PB == 0)[:, None] & (jnp.arange(NREM) == NREM - 1)[None, :]
    offset = jnp.where(first, PARTITION_COUNT - 1, offset)
    sender_partition = (home[:, None] + offset) % PARTITION_COUNT
    limit = counts[sender_partition, home[:, None]]
    slot = jax.random.randint(qkey, (NBLK, NREM), 0, 1 << 16) % limit
    slot = jnp.where(first, SEND - 1, slot)
    far = PB + sender_partition * SEND + slot
    cols = jnp.concatenate([local, far], axis=1).astype(jnp.int32)
    return (boundary, sends, cols)


def draw_node_geometry(key, part):
    boundary = pattern(key)[0]
    flags = jnp.any(boundary[:, :, None] == jnp.arange(PB)[None, None, :], axis=1).reshape(NBLK)
    region_key = jax.random.fold_in(key, 7)
    offset_key = jax.random.fold_in(key, 9)
    jitter_key = jax.random.fold_in(key, 10)
    amp_key = jax.random.fold_in(key, 8)
    regions = 0.5 + jax.random.uniform(region_key, (3, PARTITION_COUNT), jnp.float32, -0.14, 0.14)
    offsets = jax.random.uniform(offset_key, (3, NBLK), jnp.float32, -0.08, 0.08)
    home = regions[:, jnp.arange(NBLK) // PB]
    inner = home + offsets
    edge = 0.5 + 0.5 * (home - 0.5) + offsets
    centres = jnp.where(flags[None, :], edge, inner)
    jitter = jax.random.uniform(jitter_key, (3, NODES), jnp.float32, -0.28, 0.28)
    places = jnp.clip(jnp.repeat(centres, BLK, axis=1) + jitter, 0.0, 1.0)
    amps = jnp.exp(jax.random.uniform(amp_key, (1, NODES), jnp.float32, jnp.log(0.3), jnp.log(3.0)))
    return jnp.concatenate([places, amps], axis=0).astype(jnp.float32)


def draw_boundary(key, part):
    return pattern(key)[0]


def draw_sends(key, part):
    return pattern(key)[1]


def draw_cols(key, part):
    return pattern(key)[2]


def levels(key, shape, split, least, largest):
    gain, own = 1.0, jax.random.fold_in(key, 6)
    for axis_at, blocks in split:
        heights = jnp.exp(jax.random.uniform(jax.random.fold_in(own, axis_at), (blocks,), jnp.float32, least / len(split), largest / len(split)))
        gain = gain * jnp.repeat(heights, shape[axis_at] // blocks).reshape([-1 if axis == axis_at else 1 for axis in range(len(shape))])
    return gain


def normal_values(key, dims, deviation, reach, pieces=(), kind=jnp.bfloat16):
    result = deviation * jax.random.normal(key, dims, jnp.float32)
    if pieces:
        result = result * levels(key, dims, pieces, -0.22, 0.18)
    return jnp.clip(result, -reach, reach).astype(kind)


def setup_inputs(seed: int = 0, part: int = 0) -> dict:
    splits = jax.random.split(jax.random.key(seed), 7)
    own_keys = jax.random.split(jax.random.fold_in(splits[6], part), 7)
    field = normal_values(own_keys[0], (NODES, STEPS), 1.0, 6.0, ((0, 16),))
    node_geometry = draw_node_geometry(jax.random.fold_in(splits[6], 71), part)
    taps = jnp.clip(jax.random.uniform(splits[2], (2 * BAND + 1,), jnp.float32, 0.049804688, 0.19921875), 0.049804688, 0.19921875).astype(jnp.bfloat16)
    boundary = draw_boundary(jax.random.fold_in(splits[6], 71), part)
    sends = draw_sends(jax.random.fold_in(splits[6], 71), part)
    cols = draw_cols(jax.random.fold_in(splits[6], 71), part)
    return dict(field=field, node_geometry=node_geometry, taps=taps, boundary=boundary, sends=sends, cols=cols)


support_radius = 0.2

def kernel(row_geo, col_geo):
    total = jnp.zeros(col_geo.shape[:-2] + (row_geo.shape[-1], col_geo.shape[-1]), jnp.float32)
    for axis_c in range(3):
        diff = row_geo[..., axis_c, :][..., None, :, None] - col_geo[..., :, axis_c, :][..., :, None, :]
        total = total + diff * diff
    scaled = jnp.sqrt(total) / support_radius
    falloff = jnp.maximum(1.0 - scaled, 0.0)
    values = falloff ** 4 * (4.0 * scaled + 1.0)
    amps = row_geo[..., 3, :][..., None, :, None] * col_geo[..., :, 3, :][..., :, None, :]
    norm = 1.0 / math.sqrt(col_geo.shape[-3])
    return (amps * values * norm).astype(jnp.bfloat16)

def reference(field, node_geometry, taps, boundary, sends, cols):
    band = (taps.shape[0] - 1) // 2
    steps = field.shape[1]
    nblk = cols.shape[0]
    taps_wide = taps.astype(jnp.float32)
    blocks = field.reshape(nblk, BLK, steps)

    def temporal_factor(block):
        padded = jnp.pad(block.astype(jnp.float32), ((0, 0), (band, band)))
        total = jnp.zeros((BLK, steps), jnp.float32)
        for lag in range(2 * band + 1):
            total = total + taps_wide[lag] * padded[:, lag:lag + steps]
        return total.astype(jnp.bfloat16)
    filtered = lax.map(temporal_factor, blocks)
    home = (jnp.arange(nblk) // PB).astype(jnp.int32)[:, None]
    remote = jnp.maximum(cols - PB, 0)
    sender_partition = remote // SEND
    slot = remote % SEND
    position = sends[sender_partition, home, slot]
    glob = jnp.where(cols < PB, home * PB + cols, sender_partition * PB + boundary[sender_partition, position]).astype(jnp.int32)
    geo_blocks = jnp.transpose(node_geometry.reshape(4, nblk, BLK), (1, 0, 2))

    def one_row(index):
        chosen = glob[index]
        kern = kernel(geo_blocks[index], geo_blocks[chosen]).astype(jnp.float32)
        picked = filtered[chosen].astype(jnp.float32)
        return jnp.einsum('kij,kjt->it', kern, picked).astype(jnp.bfloat16)
    applied = lax.map(one_row, jnp.arange(nblk).astype(jnp.int32))
    return applied.reshape(nblk * BLK, steps)
```

```python
import functools
import math

import jax
import jax.numpy as jnp
from jax import lax
from jax.experimental import pallas as pl
from jax.experimental.pallas import tpu as pltpu
from jax.sharding import PartitionSpec as P

BLK = 128
SEND = 4
LANES = 128
MESH = pl.DeviceIdType.MESH
SUPPORT_RADIUS = 0.2


def wide_pieces(chunks):
    counts = ([1] * chunks + [1, 1, 2, 4])[-chunks:] if chunks <= 4 else [1] * (chunks - 2) + [2, 4]
    return [(c, h, counts[c]) for c in range(chunks) for h in range(counts[c])]


def wide_body(
    sizes, field, geo, taps, boundary, sends, cols, out,
    padded, table, partial, filt, geo_own, geo_stage, geo_far, kern, *rest,
):
    tm, nodes, chunks, part_blocks, nnz, nloc, own_blocks = sizes
    rest = list(rest)
    parts = wide_pieces(chunks)
    zs = [rest.pop(0) for _ in parts]
    stages = [rest.pop(0) for _ in parts]
    fars = [rest.pop(0) for _ in parts]
    outs = [rest.pop(0) for _ in range(chunks)]
    (load_sem, own_sem, out_sem, gz_send, gz_recv, gn_send, gn_recv,
     z_send, z_recv, n_send, n_recv) = rest
    me_t = lax.axis_index("tm")
    me_n = lax.axis_index("node")
    rows = own_blocks * BLK
    steps = tm * chunks * LANES

    load = pltpu.make_async_copy(field, padded.at[:, pl.ds(LANES, steps)], load_sem)
    load.start()

    barrier = pltpu.get_barrier_semaphore()
    for s in range(1, tm):
        pl.semaphore_signal(barrier, inc=1, device_id={"tm": lax.rem(me_t + s, tm)}, device_id_type=MESH)
    for s in range(1, nodes):
        pl.semaphore_signal(barrier, inc=1, device_id={"node": lax.rem(me_n + s, nodes)}, device_id_type=MESH)

    padded[:, :LANES] = jnp.zeros((rows, LANES), padded.dtype)
    padded[:, LANES + steps:] = jnp.zeros((rows, LANES), padded.dtype)
    for b in range(own_blocks):
        geo_own[pl.ds(me_t * own_blocks + b, 1), 0:4, :] = geo[:, b * BLK:(b + 1) * BLK][None]
    ntaps = taps.shape[0]
    half = (ntaps - 1) // 2
    top = LANES - half
    span = LANES + 2 * half
    lag = (
        lax.broadcasted_iota(jnp.int32, (span, LANES), 0)
        - lax.broadcasted_iota(jnp.int32, (span, LANES), 1)
    )
    table[:top, :] = jnp.zeros((top, LANES), table.dtype)
    table[top + span:, :] = jnp.zeros((top, LANES), table.dtype)
    table[top:top + span, :] = lax.fori_loop(
        0, ntaps, lambda d, acc: jnp.where(lag == d, taps[d], acc),
        jnp.zeros((span, LANES), jnp.float32),
    ).astype(table.dtype)
    pl.semaphore_wait(barrier, tm + nodes - 2)

    my_geo = geo_own.at[pl.ds(me_t * own_blocks, own_blocks)]
    gz = [
        pltpu.make_async_remote_copy(
            my_geo, my_geo, gz_send.at[s], gz_recv.at[s],
            device_id={"tm": lax.rem(me_t + s, tm)}, device_id_type=MESH)
        for s in range(1, tm)
    ]
    for copy in gz:
        copy.start()
    load.wait()

    order = sorted(range(1, tm), key=lambda s: abs(s - tm / 2))
    zc = []
    for c in range(chunks):
        for s in order + [0]:
            dest = lax.rem(me_t + s, tm)
            at = pl.multiple_of((dest * chunks + c) * LANES, LANES)
            value = jnp.dot(
                padded[:, pl.ds(at, 3 * LANES)], table[...], preferred_element_type=jnp.float32
            ).astype(jnp.bfloat16).reshape(own_blocks, BLK, LANES)
            filt[c * tm + s] = value
        for u, (_, h, count) in enumerate(parts):
            if parts[u][0] != c:
                continue
            height = BLK // count
            mine = pl.ds(me_t * own_blocks, own_blocks)
            for s in order:
                copy = pltpu.make_async_remote_copy(
                    filt.at[c * tm + s, :, pl.ds(h * height, height)],
                    zs[u].at[mine],
                    z_send.at[u * tm + s], z_recv.at[u * tm + s],
                    device_id={"tm": lax.rem(me_t + s, tm)}, device_id_type=MESH)
                if u < 2:
                    copy.start()
                zc.append((u, copy))
            zs[u][mine] = filt[c * tm, :, h * height:(h + 1) * height, :]

    def chosen(q, k):
        return boundary[0, sends[me_n, q, k]]

    for copy in gz:
        copy.wait_recv()
    gn = []
    for s in range(1, nodes):
        q = lax.rem(me_n + s, nodes)
        for k in range(SEND):
            geo_stage[s * SEND + k] = geo_own[chosen(q, k)]
        copy = pltpu.make_async_remote_copy(
            geo_stage.at[pl.ds(s * SEND, SEND)],
            geo_far.at[pl.ds((nodes - 1 - s) * SEND, SEND)],
            gn_send.at[s], gn_recv.at[s],
            device_id={"node": q}, device_id_type=MESH)
        copy.start()
        gn.append(copy)

    slots = (nodes - 1) * SEND
    dense = part_blocks <= nloc

    def far_slot(value):
        at = jnp.maximum(value - part_blocks, 0)
        src = lax.rem(at // SEND + nodes - 1 - me_n, nodes)
        return jnp.minimum(src * SEND + lax.rem(at, SEND), slots - 1)

    def build(lo, hi):
        def step(r, carry):
            mine = geo_own[r]
            spread = [
                jnp.transpose(jnp.broadcast_to(mine[axis:axis + 1], (BLK, BLK)))
                for axis in range(4)
            ]
            row = [v * (1.0 / SUPPORT_RADIUS) for v in spread[:3]]
            amp = spread[3] * (1.0 / math.sqrt(nnz))
            for g in range(lo, hi):
                if dense:
                    if g < part_blocks:
                        other, name, among = geo_own[g], g, range(nloc)
                    else:
                        rel, slot = divmod(g - part_blocks, SEND)
                        other, among = geo_far[g - part_blocks], range(nloc, nnz)
                        name = part_blocks + lax.rem(me_n + 1 + rel, nodes) * SEND + slot
                    count = 0
                    for k in among:
                        count = count + (cols[r, k] == name).astype(jnp.int32)
                    weight = other[3:4] * count.astype(jnp.float32)
                else:
                    if g < nloc:
                        other = geo_own[cols[r, g]]
                    else:
                        other = geo_far[far_slot(cols[r, g])]
                    weight = other[3:4]
                total = None
                for axis in range(3):
                    diff = row[axis] - other[axis:axis + 1] * (1.0 / SUPPORT_RADIUS)
                    total = diff * diff if total is None else total + diff * diff
                scaled = total * lax.rsqrt(jnp.maximum(total, 1e-30))
                falloff = jnp.maximum(1.0 - scaled, 0.0)
                square = falloff * falloff
                values = square * square * (4.0 * scaled + 1.0)
                kern[r, :, g * BLK:(g + 1) * BLK] = (amp * weight * values).astype(jnp.bfloat16)
            return carry
        lax.fori_loop(0, part_blocks, step, 0)

    nc = []

    ahead = {u: (u + 2,) for u in range(len(parts))}
    if len(parts) == 8:
        ahead = {0: (2, 3), 1: (4, 5), 2: (6,), 3: (7,)}

    def forward(u):
        for at, copy in zc:
            if at == u:
                copy.wait_recv()
        for at, copy in zc:
            if at in ahead.get(u, ()):
                copy.start()
        for s in range(1, nodes):
            q = lax.rem(me_n + s, nodes)
            for k in range(SEND):
                stages[u][s * SEND + k] = zs[u][chosen(q, k)]
            copy = pltpu.make_async_remote_copy(
                stages[u].at[pl.ds(s * SEND, SEND)],
                fars[u].at[pl.ds((nodes - 1 - s) * SEND, SEND)],
                n_send.at[u * nodes + s], n_recv.at[u * nodes + s],
                device_id={"node": q}, device_id_type=MESH)
            copy.start()
            nc.append((u, copy))

    outc = []

    split = part_blocks if dense else nloc
    width = part_blocks + slots if dense else nnz
    tile = own_blocks if dense else 1

    def of(c):
        return [u for u, piece in enumerate(parts) if piece[0] == c]

    def product(r, c, lo, hi):
        if dense:
            source = zs if lo == 0 else fars
            right = jnp.concatenate(
                [source[u][...] for u in of(c)], axis=1
            ).reshape((hi - lo) * BLK, LANES)
        else:
            right = jnp.concatenate([
                zs[u][cols[r, k]] if k < nloc else fars[u][far_slot(cols[r, k])]
                for k in range(lo, hi) for u in of(c)
            ], axis=0)
        left = kern[pl.ds(r * tile, tile), :, lo * BLK:hi * BLK]
        return jnp.dot(
            left.reshape(tile * BLK, (hi - lo) * BLK), right,
            preferred_element_type=jnp.float32)

    def local(c):
        def step(r, carry):
            partial[pl.ds(r * tile, tile)] = product(r, c, 0, split).reshape(tile, BLK, LANES)
            return carry
        lax.fori_loop(0, part_blocks // tile, step, 0)

    def far(c):
        for at, copy in nc:
            if parts[at][0] == c:
                copy.wait_recv()

        def step(r, carry):
            total = partial[pl.ds(r * tile, tile)].reshape(tile * BLK, LANES) + product(r, c, split, width)
            outs[c][pl.ds(pl.multiple_of(r * tile * BLK, tile * BLK), tile * BLK), :] = total.astype(jnp.bfloat16)
            return carry
        lax.fori_loop(0, part_blocks // tile, step, 0)
        copy = pltpu.make_async_copy(outs[c], out.at[:, pl.ds(c * LANES, LANES)], out_sem.at[c])
        copy.start()
        outc.append(copy)

    build(0, split)
    for u in of(0)[:1]:
        forward(u)
    for copy in gn:
        copy.wait_recv()
    build(split, width)
    for u in of(0)[1:]:
        forward(u)
    local(0)
    for c in range(1, chunks):
        todo = of(c)
        for u in todo[:-1] if len(todo) > 2 else todo[:1]:
            forward(u)
        far(c - 1)
        for u in todo[-1:] if len(todo) > 1 else []:
            forward(u)
        local(c)
    far(chunks - 1)

    for copy in gz + gn:
        copy.wait_send()
    for _, copy in zc + nc:
        copy.wait_send()
    for copy in outc:
        copy.wait()


def wide_on_device(field, node_geometry, taps, boundary, sends, cols):
    tm = lax.axis_size("tm")
    nodes = lax.axis_size("node")
    rows, steps = field.shape
    part_blocks, nnz = cols.shape
    nloc = nnz - 4
    own_blocks = rows // BLK
    chunks = steps // tm // LANES
    parts = wide_pieces(chunks)
    sizes = (tm, nodes, chunks, part_blocks, nnz, nloc, own_blocks)
    slab = part_blocks * BLK
    slots = (nodes - 1) * SEND
    width = part_blocks + slots if part_blocks <= nloc else nnz
    bf = jnp.bfloat16
    dma = pltpu.SemaphoreType.DMA
    return pl.pallas_call(
        functools.partial(wide_body, sizes),
        out_shape=pltpu.VMEM((slab, steps // tm), bf),
        in_specs=[
            pl.BlockSpec(memory_space=pl.ANY),
            pl.BlockSpec(memory_space=pltpu.VMEM),
            pl.BlockSpec(memory_space=pltpu.SMEM),
            pl.BlockSpec(memory_space=pltpu.SMEM),
            pl.BlockSpec(memory_space=pltpu.SMEM),
            pl.BlockSpec(memory_space=pltpu.SMEM),
        ],
        out_specs=pl.BlockSpec(memory_space=pltpu.VMEM),
        scratch_shapes=[
            pltpu.VMEM((rows, steps + 2 * LANES), bf),
            pltpu.VMEM((3 * LANES, LANES), bf),
            pltpu.VMEM((part_blocks, BLK, LANES), jnp.float32),
            pltpu.VMEM((chunks * tm, own_blocks, BLK, LANES), bf),
            pltpu.VMEM((part_blocks, 8, BLK), jnp.float32),
            pltpu.VMEM((nodes * SEND, 8, BLK), jnp.float32),
            pltpu.VMEM((slots, 8, BLK), jnp.float32),
            pltpu.VMEM((part_blocks, BLK, width * BLK), bf),
            *[pltpu.VMEM((part_blocks, BLK // p[2], LANES), bf) for p in parts],
            *[pltpu.VMEM((nodes * SEND, BLK // p[2], LANES), bf) for p in parts],
            *[pltpu.VMEM((slots, BLK // p[2], LANES), bf) for p in parts],
            *[pltpu.VMEM((slab, LANES), bf) for _ in range(chunks)],
            dma, dma,
            dma((chunks,)),
            dma((tm,)), dma((tm,)),
            dma((nodes,)), dma((nodes,)),
            dma((len(parts) * tm,)), dma((len(parts) * tm,)),
            dma((len(parts) * nodes,)), dma((len(parts) * nodes,)),
        ],
        compiler_params=pltpu.CompilerParams(
            collective_id=0, has_side_effects=True, vmem_limit_bytes=58 * 1024 * 1024
        ),
    )(field, node_geometry, taps.astype(jnp.float32), boundary, sends, cols)


WIN = 256


def plan(width):
    narrow = max(width // 2, LANES)
    spans = [(0, 32, 0, width), (32, 32, 0, width), (64, 32, 0, width), (96, 16, 0, width)]
    spans += [(112, 16, at, narrow) for at in range(0, width, narrow)]
    return spans


AHEAD = {0: (2,), 1: (3, 4), 2: (5,)}
FLYING = 2


def body(
    sizes, field, geo, taps, boundary, sends, cols, out,
    padded, table, partial, amps, geo_own, geo_stage, geo_far, rowmat, *rest,
):
    tm, nodes, width, part_blocks, nnz, nloc, own_blocks = sizes
    spans = plan(width)
    groups = sorted({(a, h) for a, h, _, _ in spans})
    count = len(spans)
    rest = list(rest)
    filts = [rest.pop(0) for _ in spans]
    zs = [rest.pop(0) for _ in spans]
    stages = [rest.pop(0) for _ in spans]
    fars = [rest.pop(0) for _ in spans]
    near_kern = [rest.pop(0) for _ in groups]
    far_kern = [rest.pop(0) for _ in groups]
    near_cols = [rest.pop(0) for _ in groups]
    far_cols = [rest.pop(0) for _ in groups]
    near_weight = [rest.pop(0) for _ in groups]
    far_weight = [rest.pop(0) for _ in groups]
    load_sem, gz_send, gz_recv, gn_send, gn_recv, z_send, z_recv, n_send, n_recv = rest
    me_t = lax.axis_index("tm")
    me_n = lax.axis_index("node")
    steps = tm * width
    slots = (nodes - 1) * SEND
    f32, bf = jnp.float32, jnp.bfloat16

    loads = {}
    for i, (a, h) in enumerate(groups):
        loads[a] = pltpu.make_async_copy(
            field.at[:, pl.ds(a, h)], padded.at[:, pl.ds(a, h), pl.ds(LANES, steps)], load_sem.at[i])
        loads[a].start()

    barrier = pltpu.get_barrier_semaphore()
    for s in range(1, tm):
        pl.semaphore_signal(barrier, inc=1, device_id={"tm": lax.rem(me_t + s, tm)}, device_id_type=MESH)
    for s in range(1, nodes):
        pl.semaphore_signal(barrier, inc=1, device_id={"node": lax.rem(me_n + s, nodes)}, device_id_type=MESH)

    padded[:, :, :LANES] = jnp.zeros((own_blocks, BLK, LANES), bf)
    padded[:, :, LANES + steps:] = jnp.zeros((own_blocks, BLK, LANES), bf)
    for b in range(own_blocks):
        geo_own[pl.ds(me_t * own_blocks + b, 1), 0:4, :] = geo[:, b * BLK:(b + 1) * BLK][None]

    ntaps = taps.shape[0]
    half = (ntaps - 1) // 2
    top = LANES - half
    line = jnp.concatenate(
        [taps[...].astype(f32).reshape(1, ntaps), jnp.zeros((1, 2 * LANES - ntaps), f32)], axis=1)
    slanted = pltpu.roll(jnp.broadcast_to(line, (LANES, 2 * LANES)), 0, 1, stride=1, stride_axis=0)
    toeplitz = jnp.transpose(slanted).astype(bf)
    table[...] = jnp.zeros(table.shape, bf)
    for w in range(WIN // LANES):
        table[top + w * LANES:top + (w + 2) * LANES, w * LANES:(w + 1) * LANES] = toeplitz

    order = sorted(range(1, tm), key=lambda s: abs(s - tm / 2))
    zc = {}

    def partner(s):
        return lax.rem(me_t + s, tm)

    mine = pl.ds(me_t * own_blocks, own_blocks)

    def filtering(u):
        a, h, c0, cw = spans[u]
        for s in order + [0]:
            dest = partner(s)
            for w in range(0, cw, WIN):
                n = min(WIN, cw - w)
                at = pl.multiple_of(dest * width + c0 + w, LANES)
                window = padded[:, a:a + h, pl.ds(at, n + 2 * LANES)].reshape(own_blocks * h, n + 2 * LANES)
                value = jnp.dot(window, table[:n + 2 * LANES, :n], preferred_element_type=f32)
                value = value.astype(bf).reshape(own_blocks, h, n)
                if s:
                    filts[u][s - 1, :, :, w:w + n] = value
                else:
                    zs[u][mine, :, w:w + n] = value
        zc[u] = [
            pltpu.make_async_remote_copy(
                filts[u].at[s - 1], zs[u].at[mine],
                z_send.at[u * tm + s], z_recv.at[u * tm + s],
                device_id={"tm": partner(s)}, device_id_type=MESH)
            for s in order
        ]

    for u in range(1):
        loads[spans[u][0]].wait()
        filtering(u)
    pl.semaphore_wait(barrier, tm + nodes - 2)
    my_geo = geo_own.at[mine]
    gz = [
        pltpu.make_async_remote_copy(
            my_geo, my_geo, gz_send.at[s], gz_recv.at[s],
            device_id={"tm": partner(s)}, device_id_type=MESH)
        for s in order
    ]
    for copy in gz:
        copy.start()
    for copy in zc[0]:
        copy.start()
    waited = {spans[0][0]}
    for u in range(1, count):
        if spans[u][0] not in waited:
            loads[spans[u][0]].wait()
            waited.add(spans[u][0])
        filtering(u)
        if u < FLYING:
            for copy in zc[u]:
                copy.start()

    def chosen(q, k):
        return boundary[0, sends[me_n, q, k]]

    for copy in gz:
        copy.wait_recv()
    gn = []
    for s in range(1, nodes):
        q = lax.rem(me_n + s, nodes)
        for k in range(SEND):
            geo_stage[s * SEND + k] = geo_own[chosen(q, k)]
        copy = pltpu.make_async_remote_copy(
            geo_stage.at[pl.ds(s * SEND, SEND)],
            geo_far.at[pl.ds((nodes - 1 - s) * SEND, SEND)],
            gn_send.at[s], gn_recv.at[s],
            device_id={"node": q}, device_id_type=MESH)
        copy.start()
        gn.append(copy)

    def halves(value):
        high = value.astype(bf).astype(f32)
        rest = value - high
        middle = rest.astype(bf).astype(f32)
        return high, middle, rest - middle

    def scaled(block):
        row = lax.broadcasted_iota(jnp.int32, block.shape, 0)
        point = jnp.where(row < 3, (block - 0.5) * (1.0 / SUPPORT_RADIUS), 0.0)
        norm = jnp.broadcast_to(jnp.sum(point * point, axis=0, keepdims=True), block.shape)
        return row, point, norm

    def left(block):
        row, point, norm = scaled(block)
        high, middle, low = halves(jnp.where(row < 3, -2.0 * point, jnp.where(row == 3, norm, jnp.where(row == 4, 1.0, 0.0))))
        return jnp.concatenate([high, high, middle, middle, high, low], axis=0)

    def right(block):
        row, point, norm = scaled(block)
        high, middle, low = halves(jnp.where(row < 3, point, jnp.where(row == 3, 1.0, jnp.where(row == 4, norm, 0.0))))
        return jnp.concatenate([high, middle, high, middle, low, high], axis=0)

    def row_step(r, carry):
        block = geo_own[r]
        at = pl.ds(pl.multiple_of(r * BLK, BLK), BLK)
        rowmat[at, :] = jnp.transpose(left(block)).astype(bf)
        amps[at, :] = jnp.transpose(jnp.broadcast_to(block[3:4] * (1.0 / math.sqrt(nnz)), (BLK, BLK)))
        return carry

    def prepare(i, is_far):
        a, h = groups[i]
        source, blocks = (geo_far, slots) if is_far else (geo_own, part_blocks)
        joined = jnp.concatenate([source[g, :, a:a + h] for g in range(blocks)], axis=1)
        (far_cols if is_far else near_cols)[i][...] = right(joined).astype(bf)
        lane = lax.broadcasted_iota(jnp.int32, (part_blocks, blocks * h), 1)
        name = lax.shift_right_logical(lane, h.bit_length() - 1)
        if is_far:
            owner = me_n + 1 + lax.shift_right_logical(name, 2)
            owner = jnp.where(owner >= nodes, owner - nodes, owner)
            name = part_blocks + owner * SEND + jnp.bitwise_and(name, SEND - 1)
        total = jnp.zeros(name.shape, f32)
        for k in range(nloc, nnz) if is_far else range(nloc):
            total = total + jnp.where(cols[:, k:k + 1] == name, 1.0, 0.0)
        weight = total * joined[3:4]
        (far_weight if is_far else near_weight)[i][...] = weight

    def build(i, is_far):
        column = (far_cols if is_far else near_cols)[i]
        weights = (far_weight if is_far else near_weight)[i]
        target = (far_kern if is_far else near_kern)[i]

        def step(r, carry):
            at = pl.ds(pl.multiple_of(r * BLK, BLK), BLK)
            square = jnp.dot(rowmat[at, :], column[...], preferred_element_type=f32)
            square = jnp.maximum(square, 1e-30)
            falloff = jnp.maximum(1.0 - square * lax.rsqrt(square), 0.0)
            power = falloff * falloff
            weight = weights[pl.ds(r, 1), :]
            target[at, :] = (power * power * (5.0 * weight - (4.0 * weight) * falloff)).astype(bf)
            return carry
        lax.fori_loop(0, part_blocks, step, 0)

    nc = {}

    def forward(u):
        for copy in zc[u]:
            copy.wait_recv()
        for v in AHEAD.get(u, ()):
            if v < count:
                for copy in zc[v]:
                    copy.start()
        nc[u] = []
        for s in range(1, nodes):
            q = lax.rem(me_n + s, nodes)
            for k in range(SEND):
                stages[u][s * SEND + k] = zs[u][chosen(q, k)]
            copy = pltpu.make_async_remote_copy(
                stages[u].at[pl.ds(s * SEND, SEND)],
                fars[u].at[pl.ds((nodes - 1 - s) * SEND, SEND)],
                n_send.at[u * nodes + s], n_recv.at[u * nodes + s],
                device_id={"node": q}, device_id_type=MESH)
            copy.start()
            nc[u].append(copy)

    tile = own_blocks * BLK

    def add(terms, c0, cw, first=False, last=False):
        for is_far, u in terms:
            if is_far:
                for copy in nc[u]:
                    copy.wait_recv()

        def step(r, carry):
            at = pl.ds(pl.multiple_of(r * tile, tile), tile)
            total = None if first else partial[at, c0:c0 + cw]
            for is_far, u in terms:
                a, h, p0, pw = spans[u]
                source = (fars if is_far else zs)[u]
                i = groups.index((a, h))
                kern = (far_kern if is_far else near_kern)[i]
                blocks = source.shape[0]
                term = jnp.dot(
                    kern[at, :], source[:, :, c0 - p0:c0 - p0 + cw].reshape(blocks * h, cw),
                    preferred_element_type=f32)
                total = term if total is None else total + term
            if last:
                scale = jnp.concatenate([amps[at, :]] * (cw // LANES), axis=1)
                out[at, c0:c0 + cw] = (total * scale).astype(bf)
            else:
                partial[at, c0:c0 + cw] = total
            return carry
        lax.fori_loop(0, part_blocks // own_blocks, step, 0)

    lax.fori_loop(0, part_blocks, row_step, 0)
    for i in range(len(groups)):
        prepare(i, False)
    for i in range(len(groups)):
        build(i, False)
    forward(0)
    for copy in gn:
        copy.wait_recv()
    for i in range(len(groups)):
        prepare(i, True)
    for i in range(len(groups)):
        build(i, True)
    add([(False, 0)], 0, width, first=True)
    forward(1)
    add([(False, 1), (True, 0)], 0, width)
    forward(2)
    add([(False, 2), (True, 1)], 0, width)
    forward(3)
    add([(False, 3), (True, 2)], 0, width)
    narrow = spans[4:]
    forward(4)
    add([(False, 4)], *narrow[0][2:])
    for u in range(5, count):
        forward(u)
        add([(False, u)], *spans[u][2:])
    add([(True, 3)], 0, width)
    for u in range(4, count):
        add([(True, u)], *spans[u][2:], last=True)

    for copy in gz + gn:
        copy.wait_send()
    for u in range(count):
        for copy in zc[u] + nc[u]:
            copy.wait_send()


def on_device(field, node_geometry, taps, boundary, sends, cols):
    tm = lax.axis_size("tm")
    nodes = lax.axis_size("node")
    rows, steps = field.shape
    part_blocks, nnz = cols.shape
    nloc = nnz - 4
    if part_blocks > nloc:
        return wide_on_device(field, node_geometry, taps, boundary, sends, cols)
    own_blocks = rows // BLK
    width = steps // tm
    sizes = (tm, nodes, width, part_blocks, nnz, nloc, own_blocks)
    spans = plan(width)
    groups = sorted({(a, h) for a, h, _, _ in spans})
    count = len(spans)
    slab = part_blocks * BLK
    slots = (nodes - 1) * SEND
    bf, f32 = jnp.bfloat16, jnp.float32
    dma = pltpu.SemaphoreType.DMA
    vmem = pl.BlockSpec(memory_space=pltpu.VMEM)
    smem = pl.BlockSpec(memory_space=pltpu.SMEM)
    return pl.pallas_call(
        functools.partial(body, sizes),
        out_shape=pltpu.VMEM((slab, width), bf),
        in_specs=[pl.BlockSpec(memory_space=pl.ANY), vmem, vmem, smem, smem, vmem],
        out_specs=vmem,
        scratch_shapes=[
            pltpu.VMEM((own_blocks, BLK, steps + 2 * LANES), bf),
            pltpu.VMEM((WIN + 2 * LANES, WIN), bf),
            pltpu.VMEM((slab, width), f32),
            pltpu.VMEM((slab, LANES), f32),
            pltpu.VMEM((part_blocks, 8, BLK), f32),
            pltpu.VMEM((nodes * SEND, 8, BLK), f32),
            pltpu.VMEM((slots, 8, BLK), f32),
            pltpu.VMEM((slab, 48), bf),
            *[pltpu.VMEM((tm - 1, own_blocks, h, cw), bf) for _, h, _, cw in spans],
            *[pltpu.VMEM((part_blocks, h, cw), bf) for _, h, _, cw in spans],
            *[pltpu.VMEM((nodes * SEND, h, cw), bf) for _, h, _, cw in spans],
            *[pltpu.VMEM((slots, h, cw), bf) for _, h, _, cw in spans],
            *[pltpu.VMEM((slab, part_blocks * h), bf) for _, h in groups],
            *[pltpu.VMEM((slab, slots * h), bf) for _, h in groups],
            *[pltpu.VMEM((48, part_blocks * h), bf) for _, h in groups],
            *[pltpu.VMEM((48, slots * h), bf) for _, h in groups],
            *[pltpu.VMEM((part_blocks, part_blocks * h), f32) for _, h in groups],
            *[pltpu.VMEM((part_blocks, slots * h), f32) for _, h in groups],
            dma((len(groups),)),
            dma((tm,)), dma((tm,)),
            dma((nodes,)), dma((nodes,)),
            dma((count * tm,)), dma((count * tm,)),
            dma((count * nodes,)), dma((count * nodes,)),
        ],
        compiler_params=pltpu.CompilerParams(
            collective_id=0, has_side_effects=True, vmem_limit_bytes=58 * 1024 * 1024
        ),
    )(field.reshape(own_blocks, BLK, steps), node_geometry, taps, boundary, sends, cols)


def solution(mesh):
    return jax.shard_map(
        on_device,
        mesh=mesh,
        in_specs=(
            P(("parts", "node", "tm"), None),
            P(None, ("node", "tm")),
            P(),
            P("node", None),
            P(),
            P("node", None),
        ),
        out_specs=P(("parts", "node"), "tm"),
        check_vma=False,
    )
```

```python
import functools
import math

import jax
import jax.numpy as jnp
from jax import lax
from jax.experimental import pallas as pl
from jax.experimental.pallas import tpu as pltpu
from jax.sharding import PartitionSpec as P

BLK = 128
SEND = 4
LANES = 128
MESH = pl.DeviceIdType.MESH
SUPPORT_RADIUS = 0.2


def wide_pieces(chunks):
    counts = ([1] * chunks + [1, 1, 2, 4])[-chunks:] if chunks <= 4 else [1] * (chunks - 2) + [2, 4]
    return [(c, h, counts[c]) for c in range(chunks) for h in range(counts[c])]


def wide_body(
    sizes, field, geo, taps, boundary, sends, cols, out,
    padded, table, partial, filt, geo_own, geo_stage, geo_far, kern, *rest,
):
    tm, nodes, chunks, part_blocks, nnz, nloc, own_blocks = sizes
    rest = list(rest)
    parts = wide_pieces(chunks)
    zs = [rest.pop(0) for _ in parts]
    stages = [rest.pop(0) for _ in parts]
    fars = [rest.pop(0) for _ in parts]
    outs = [rest.pop(0) for _ in range(chunks)]
    (load_sem, own_sem, out_sem, gz_send, gz_recv, gn_send, gn_recv,
     z_send, z_recv, n_send, n_recv) = rest
    me_t = lax.axis_index("tm")
    me_n = lax.axis_index("node")
    rows = own_blocks * BLK
    steps = tm * chunks * LANES

    load = pltpu.make_async_copy(field, padded.at[:, pl.ds(LANES, steps)], load_sem)
    load.start()

    barrier = pltpu.get_barrier_semaphore()
    for s in range(1, tm):
        pl.semaphore_signal(barrier, inc=1, device_id={"tm": lax.rem(me_t + s, tm)}, device_id_type=MESH)
    for s in range(1, nodes):
        pl.semaphore_signal(barrier, inc=1, device_id={"node": lax.rem(me_n + s, nodes)}, device_id_type=MESH)

    padded[:, :LANES] = jnp.zeros((rows, LANES), padded.dtype)
    padded[:, LANES + steps:] = jnp.zeros((rows, LANES), padded.dtype)
    for b in range(own_blocks):
        geo_own[pl.ds(me_t * own_blocks + b, 1), 0:4, :] = geo[:, b * BLK:(b + 1) * BLK][None]
    ntaps = taps.shape[0]
    half = (ntaps - 1) // 2
    top = LANES - half
    span = LANES + 2 * half
    lag = (
        lax.broadcasted_iota(jnp.int32, (span, LANES), 0)
        - lax.broadcasted_iota(jnp.int32, (span, LANES), 1)
    )
    table[:top, :] = jnp.zeros((top, LANES), table.dtype)
    table[top + span:, :] = jnp.zeros((top, LANES), table.dtype)
    table[top:top + span, :] = lax.fori_loop(
        0, ntaps, lambda d, acc: jnp.where(lag == d, taps[d], acc),
        jnp.zeros((span, LANES), jnp.float32),
    ).astype(table.dtype)
    pl.semaphore_wait(barrier, tm + nodes - 2)

    my_geo = geo_own.at[pl.ds(me_t * own_blocks, own_blocks)]
    gz = [
        pltpu.make_async_remote_copy(
            my_geo, my_geo, gz_send.at[s], gz_recv.at[s],
            device_id={"tm": lax.rem(me_t + s, tm)}, device_id_type=MESH)
        for s in range(1, tm)
    ]
    for copy in gz:
        copy.start()
    load.wait()

    order = sorted(range(1, tm), key=lambda s: abs(s - tm / 2))
    zc = []
    for c in range(chunks):
        for s in order + [0]:
            dest = lax.rem(me_t + s, tm)
            at = pl.multiple_of((dest * chunks + c) * LANES, LANES)
            value = jnp.dot(
                padded[:, pl.ds(at, 3 * LANES)], table[...], preferred_element_type=jnp.float32
            ).astype(jnp.bfloat16).reshape(own_blocks, BLK, LANES)
            filt[c * tm + s] = value
        for u, (_, h, count) in enumerate(parts):
            if parts[u][0] != c:
                continue
            height = BLK // count
            mine = pl.ds(me_t * own_blocks, own_blocks)
            for s in order:
                copy = pltpu.make_async_remote_copy(
                    filt.at[c * tm + s, :, pl.ds(h * height, height)],
                    zs[u].at[mine],
                    z_send.at[u * tm + s], z_recv.at[u * tm + s],
                    device_id={"tm": lax.rem(me_t + s, tm)}, device_id_type=MESH)
                if u < 2:
                    copy.start()
                zc.append((u, copy))
            zs[u][mine] = filt[c * tm, :, h * height:(h + 1) * height, :]

    def chosen(q, k):
        return boundary[0, sends[me_n, q, k]]

    for copy in gz:
        copy.wait_recv()
    gn = []
    for s in range(1, nodes):
        q = lax.rem(me_n + s, nodes)
        for k in range(SEND):
            geo_stage[s * SEND + k] = geo_own[chosen(q, k)]
        copy = pltpu.make_async_remote_copy(
            geo_stage.at[pl.ds(s * SEND, SEND)],
            geo_far.at[pl.ds((nodes - 1 - s) * SEND, SEND)],
            gn_send.at[s], gn_recv.at[s],
            device_id={"node": q}, device_id_type=MESH)
        copy.start()
        gn.append(copy)

    slots = (nodes - 1) * SEND
    dense = part_blocks <= nloc

    def far_slot(value):
        at = jnp.maximum(value - part_blocks, 0)
        src = lax.rem(at // SEND + nodes - 1 - me_n, nodes)
        return jnp.minimum(src * SEND + lax.rem(at, SEND), slots - 1)

    def build(lo, hi):
        def step(r, carry):
            mine = geo_own[r]
            spread = [
                jnp.transpose(jnp.broadcast_to(mine[axis:axis + 1], (BLK, BLK)))
                for axis in range(4)
            ]
            row = [v * (1.0 / SUPPORT_RADIUS) for v in spread[:3]]
            amp = spread[3] * (1.0 / math.sqrt(nnz))
            for g in range(lo, hi):
                if dense:
                    if g < part_blocks:
                        other, name, among = geo_own[g], g, range(nloc)
                    else:
                        rel, slot = divmod(g - part_blocks, SEND)
                        other, among = geo_far[g - part_blocks], range(nloc, nnz)
                        name = part_blocks + lax.rem(me_n + 1 + rel, nodes) * SEND + slot
                    count = 0
                    for k in among:
                        count = count + (cols[r, k] == name).astype(jnp.int32)
                    weight = other[3:4] * count.astype(jnp.float32)
                else:
                    if g < nloc:
                        other = geo_own[cols[r, g]]
                    else:
                        other = geo_far[far_slot(cols[r, g])]
                    weight = other[3:4]
                total = None
                for axis in range(3):
                    diff = row[axis] - other[axis:axis + 1] * (1.0 / SUPPORT_RADIUS)
                    total = diff * diff if total is None else total + diff * diff
                scaled = total * lax.rsqrt(jnp.maximum(total, 1e-30))
                falloff = jnp.maximum(1.0 - scaled, 0.0)
                square = falloff * falloff
                values = square * square * (4.0 * scaled + 1.0)
                kern[r, :, g * BLK:(g + 1) * BLK] = (amp * weight * values).astype(jnp.bfloat16)
            return carry
        lax.fori_loop(0, part_blocks, step, 0)

    nc = []

    ahead = {u: (u + 2,) for u in range(len(parts))}
    if len(parts) == 8:
        ahead = {0: (2, 3), 1: (4, 5), 2: (6,), 3: (7,)}

    def forward(u):
        for at, copy in zc:
            if at == u:
                copy.wait_recv()
        for at, copy in zc:
            if at in ahead.get(u, ()):
                copy.start()
        for s in range(1, nodes):
            q = lax.rem(me_n + s, nodes)
            for k in range(SEND):
                stages[u][s * SEND + k] = zs[u][chosen(q, k)]
            copy = pltpu.make_async_remote_copy(
                stages[u].at[pl.ds(s * SEND, SEND)],
                fars[u].at[pl.ds((nodes - 1 - s) * SEND, SEND)],
                n_send.at[u * nodes + s], n_recv.at[u * nodes + s],
                device_id={"node": q}, device_id_type=MESH)
            copy.start()
            nc.append((u, copy))

    outc = []

    split = part_blocks if dense else nloc
    width = part_blocks + slots if dense else nnz
    tile = own_blocks if dense else 1

    def of(c):
        return [u for u, piece in enumerate(parts) if piece[0] == c]

    def product(r, c, lo, hi):
        if dense:
            source = zs if lo == 0 else fars
            right = jnp.concatenate(
                [source[u][...] for u in of(c)], axis=1
            ).reshape((hi - lo) * BLK, LANES)
        else:
            right = jnp.concatenate([
                zs[u][cols[r, k]] if k < nloc else fars[u][far_slot(cols[r, k])]
                for k in range(lo, hi) for u in of(c)
            ], axis=0)
        left = kern[pl.ds(r * tile, tile), :, lo * BLK:hi * BLK]
        return jnp.dot(
            left.reshape(tile * BLK, (hi - lo) * BLK), right,
            preferred_element_type=jnp.float32)

    def local(c):
        def step(r, carry):
            partial[pl.ds(r * tile, tile)] = product(r, c, 0, split).reshape(tile, BLK, LANES)
            return carry
        lax.fori_loop(0, part_blocks // tile, step, 0)

    def far(c):
        for at, copy in nc:
            if parts[at][0] == c:
                copy.wait_recv()

        def step(r, carry):
            total = partial[pl.ds(r * tile, tile)].reshape(tile * BLK, LANES) + product(r, c, split, width)
            outs[c][pl.ds(pl.multiple_of(r * tile * BLK, tile * BLK), tile * BLK), :] = total.astype(jnp.bfloat16)
            return carry
        lax.fori_loop(0, part_blocks // tile, step, 0)
        copy = pltpu.make_async_copy(outs[c], out.at[:, pl.ds(c * LANES, LANES)], out_sem.at[c])
        copy.start()
        outc.append(copy)

    build(0, split)
    for u in of(0)[:1]:
        forward(u)
    for copy in gn:
        copy.wait_recv()
    build(split, width)
    for u in of(0)[1:]:
        forward(u)
    local(0)
    for c in range(1, chunks):
        todo = of(c)
        for u in todo[:-1] if len(todo) > 2 else todo[:1]:
            forward(u)
        far(c - 1)
        for u in todo[-1:] if len(todo) > 1 else []:
            forward(u)
        local(c)
    far(chunks - 1)

    for copy in gz + gn:
        copy.wait_send()
    for _, copy in zc + nc:
        copy.wait_send()
    for copy in outc:
        copy.wait()


def wide_on_device(field, node_geometry, taps, boundary, sends, cols):
    tm = lax.axis_size("tm")
    nodes = lax.axis_size("node")
    rows, steps = field.shape
    part_blocks, nnz = cols.shape
    nloc = nnz - 4
    own_blocks = rows // BLK
    chunks = steps // tm // LANES
    parts = wide_pieces(chunks)
    sizes = (tm, nodes, chunks, part_blocks, nnz, nloc, own_blocks)
    slab = part_blocks * BLK
    slots = (nodes - 1) * SEND
    width = part_blocks + slots if part_blocks <= nloc else nnz
    bf = jnp.bfloat16
    dma = pltpu.SemaphoreType.DMA
    return pl.pallas_call(
        functools.partial(wide_body, sizes),
        out_shape=pltpu.VMEM((slab, steps // tm), bf),
        in_specs=[
            pl.BlockSpec(memory_space=pl.ANY),
            pl.BlockSpec(memory_space=pltpu.VMEM),
            pl.BlockSpec(memory_space=pltpu.SMEM),
            pl.BlockSpec(memory_space=pltpu.SMEM),
            pl.BlockSpec(memory_space=pltpu.SMEM),
            pl.BlockSpec(memory_space=pltpu.SMEM),
        ],
        out_specs=pl.BlockSpec(memory_space=pltpu.VMEM),
        scratch_shapes=[
            pltpu.VMEM((rows, steps + 2 * LANES), bf),
            pltpu.VMEM((3 * LANES, LANES), bf),
            pltpu.VMEM((part_blocks, BLK, LANES), jnp.float32),
            pltpu.VMEM((chunks * tm, own_blocks, BLK, LANES), bf),
            pltpu.VMEM((part_blocks, 8, BLK), jnp.float32),
            pltpu.VMEM((nodes * SEND, 8, BLK), jnp.float32),
            pltpu.VMEM((slots, 8, BLK), jnp.float32),
            pltpu.VMEM((part_blocks, BLK, width * BLK), bf),
            *[pltpu.VMEM((part_blocks, BLK // p[2], LANES), bf) for p in parts],
            *[pltpu.VMEM((nodes * SEND, BLK // p[2], LANES), bf) for p in parts],
            *[pltpu.VMEM((slots, BLK // p[2], LANES), bf) for p in parts],
            *[pltpu.VMEM((slab, LANES), bf) for _ in range(chunks)],
            dma, dma,
            dma((chunks,)),
            dma((tm,)), dma((tm,)),
            dma((nodes,)), dma((nodes,)),
            dma((len(parts) * tm,)), dma((len(parts) * tm,)),
            dma((len(parts) * nodes,)), dma((len(parts) * nodes,)),
        ],
        compiler_params=pltpu.CompilerParams(
            collective_id=0, has_side_effects=True, vmem_limit_bytes=58 * 1024 * 1024
        ),
    )(field, node_geometry, taps.astype(jnp.float32), boundary, sends, cols)


WIN = 256


TALL = 32


def plan(width):
    quarter = max(width // 4, LANES)
    spans = [(a, 0, width) for a in range(0, BLK - TALL, TALL)]
    spans += [(BLK - TALL, 0, 2 * quarter)]
    spans += [(BLK - TALL, at, quarter) for at in range(2 * quarter, width, quarter)]
    return spans


AHEAD = {0: (2,), 1: (3,), 2: (4,), 3: (5,)}
FLYING = 2


def body(
    sizes, field, geo_in, taps_in, boundary_in, sends_in, cols_in, out,
    geo, taps, boundary, sends, cols, padded, table, partial, amps, geo_own, geo_stage, geo_far, rowmat, *rest,
):
    tm, nodes, width, part_blocks, nnz, nloc, own_blocks = sizes
    spans = plan(width)
    groups = range(0, BLK, TALL)
    count = len(spans)
    rest = list(rest)
    filts = [rest.pop(0) for _ in spans]
    zs = [rest.pop(0) for _ in spans]
    stages = [rest.pop(0) for _ in spans]
    fars = [rest.pop(0) for _ in spans]
    (near_kern, far_kern, near_cols, far_cols, near_weight, far_weight, small_sem, load_sem, gz_send, gz_recv, gn_send, gn_recv, z_send, z_recv, n_send, n_recv) = rest
    me_t = lax.axis_index("tm")
    me_n = lax.axis_index("node")
    steps = tm * width
    slots = (nodes - 1) * SEND
    f32, bf = jnp.float32, jnp.bfloat16

    barrier = pltpu.get_barrier_semaphore()
    for s in range(1, tm):
        pl.semaphore_signal(barrier, inc=1, device_id={"tm": lax.rem(me_t + s, tm)}, device_id_type=MESH)
    for s in range(1, nodes):
        pl.semaphore_signal(barrier, inc=1, device_id={"node": lax.rem(me_n + s, nodes)}, device_id_type=MESH)

    small = [
        pltpu.make_async_copy(source, target, small_sem.at[i])
        for i, (source, target) in enumerate((
            (taps_in, taps), (geo_in, geo), (boundary_in, boundary), (sends_in, sends), (cols_in, cols)))
    ]
    for copy in small[:1]:
        copy.start()
    loads = {}
    for i, a in enumerate(groups):
        loads[a] = pltpu.make_async_copy(
            field.at[:, pl.ds(a, TALL)], padded.at[:, pl.ds(a, TALL), pl.ds(LANES, steps)], load_sem.at[i])
        loads[a].start()
    for copy in small[1:]:
        copy.start()

    padded[:, :, :LANES] = jnp.zeros((own_blocks, BLK, LANES), bf)
    padded[:, :, LANES + steps:] = jnp.zeros((own_blocks, BLK, LANES), bf)
    table[...] = jnp.zeros(table.shape, bf)
    small[0].wait()
    small[1].wait()
    for b in range(own_blocks):
        geo_own[pl.ds(me_t * own_blocks + b, 1), 0:4, :] = geo[:, b * BLK:(b + 1) * BLK][None]

    ntaps = taps.shape[0]
    half = (ntaps - 1) // 2
    top = LANES - half
    line = jnp.concatenate(
        [taps[...].astype(f32).reshape(1, ntaps), jnp.zeros((1, 2 * LANES - ntaps), f32)], axis=1)
    slanted = pltpu.roll(jnp.broadcast_to(line, (LANES, 2 * LANES)), 0, 1, stride=1, stride_axis=0)
    toeplitz = jnp.transpose(slanted).astype(bf)
    for w in range(WIN // LANES):
        table[top + w * LANES:top + (w + 2) * LANES, w * LANES:(w + 1) * LANES] = toeplitz

    order = sorted(range(1, tm), key=lambda s: abs(s - tm / 2))
    zc = {}

    def partner(s):
        return lax.rem(me_t + s, tm)

    mine = pl.ds(me_t * own_blocks, own_blocks)

    def filtering(u):
        a, c0, cw = spans[u]
        for s in order + [0]:
            dest = partner(s)
            for w in range(0, cw, WIN):
                n = min(WIN, cw - w)
                at = pl.multiple_of(dest * width + c0 + w, LANES)
                window = padded[:, a:a + TALL, pl.ds(at, n + 2 * LANES)].reshape(own_blocks * TALL, n + 2 * LANES)
                value = jnp.dot(window, table[:n + 2 * LANES, :n], preferred_element_type=f32)
                value = value.astype(bf).reshape(own_blocks, TALL, n)
                if s:
                    filts[u][s - 1, :, :, w:w + n] = value
                else:
                    zs[u][mine, :, w:w + n] = value
        zc[u] = [
            pltpu.make_async_remote_copy(
                filts[u].at[s - 1], zs[u].at[mine],
                z_send.at[u * tm + s], z_recv.at[u * tm + s],
                device_id={"tm": partner(s)}, device_id_type=MESH)
            for s in order
        ]

    for u in range(1):
        loads[spans[u][0]].wait()
        filtering(u)
    pl.semaphore_wait(barrier, tm + nodes - 2)
    my_geo = geo_own.at[mine]
    gz = [
        pltpu.make_async_remote_copy(
            my_geo, my_geo, gz_send.at[s], gz_recv.at[s],
            device_id={"tm": partner(s)}, device_id_type=MESH)
        for s in order
    ]
    for copy in gz:
        copy.start()
    for copy in zc[0]:
        copy.start()
    waited = {spans[0][0]}
    for u in range(1, count):
        if spans[u][0] not in waited:
            loads[spans[u][0]].wait()
            waited.add(spans[u][0])
        filtering(u)
        if u < FLYING:
            for copy in zc[u]:
                copy.start()

    for copy in small[2:]:
        copy.wait()

    def chosen(q, k):
        return boundary[0, sends[me_n, q, k]]

    for copy in gz:
        copy.wait_recv()
    gn = []
    for s in range(1, nodes):
        q = lax.rem(me_n + s, nodes)
        for k in range(SEND):
            geo_stage[s * SEND + k] = geo_own[chosen(q, k)]
        copy = pltpu.make_async_remote_copy(
            geo_stage.at[pl.ds(s * SEND, SEND)],
            geo_far.at[pl.ds((nodes - 1 - s) * SEND, SEND)],
            gn_send.at[s], gn_recv.at[s],
            device_id={"node": q}, device_id_type=MESH)
        copy.start()
        gn.append(copy)

    tile = own_blocks * BLK

    def halves(value):
        high = value.astype(bf).astype(f32)
        rest = value - high
        middle = rest.astype(bf).astype(f32)
        return high, middle, rest - middle

    def scaled(block):
        row = lax.broadcasted_iota(jnp.int32, block.shape, 0)
        point = jnp.where(row < 3, (block - 0.5) * (1.0 / SUPPORT_RADIUS), 0.0)
        norm = jnp.broadcast_to(jnp.sum(point * point, axis=0, keepdims=True), block.shape)
        return row, point, norm

    def left(block):
        row, point, norm = scaled(block)
        high, middle, low = halves(jnp.where(row < 3, -2.0 * point, jnp.where(row == 3, norm, jnp.where(row == 4, 1.0, 0.0))))
        return jnp.concatenate([high, high, middle, middle, high, low], axis=0)

    def right(block):
        row, point, norm = scaled(block)
        high, middle, low = halves(jnp.where(row < 3, point, jnp.where(row == 3, 1.0, jnp.where(row == 4, norm, 0.0))))
        return jnp.concatenate([high, middle, high, middle, low, high], axis=0)

    def row_step(r, carry):
        block = geo_own[r]
        at = pl.ds(pl.multiple_of(r * BLK, BLK), BLK)
        rowmat[at, :] = jnp.transpose(left(block)).astype(bf)
        amps[at, :] = jnp.transpose(jnp.broadcast_to(block[3:4] * (1.0 / math.sqrt(nnz)), (BLK, BLK)))
        return carry

    def prepare(is_far):
        source, blocks = (geo_far, slots) if is_far else (geo_own, part_blocks)
        joined = jnp.concatenate([source[g, :, a:a + TALL] for a in groups for g in range(blocks)], axis=1)
        (far_cols if is_far else near_cols)[...] = right(joined).astype(bf)
        lane = lax.broadcasted_iota(jnp.int32, (part_blocks, blocks * TALL), 1)
        name = lax.shift_right_logical(lane, TALL.bit_length() - 1)
        if is_far:
            owner = me_n + 1 + lax.shift_right_logical(name, 2)
            owner = jnp.where(owner >= nodes, owner - nodes, owner)
            name = part_blocks + owner * SEND + jnp.bitwise_and(name, SEND - 1)
        total = jnp.zeros(name.shape, f32)
        for k in range(nloc, nnz) if is_far else range(nloc):
            total = total + jnp.where(cols[:, k:k + 1] == name, 1.0, 0.0)
        total = jnp.concatenate([total] * len(groups), axis=1)
        (far_weight if is_far else near_weight)[...] = total * joined[3:4]

    def build(is_far):
        column = far_cols if is_far else near_cols
        weights = far_weight if is_far else near_weight
        target = far_kern if is_far else near_kern

        def step(t, carry):
            at = pl.ds(pl.multiple_of(t * tile, tile), tile)
            for lo in range(0, column.shape[1], 3 * LANES):
                part = slice(lo, min(lo + 3 * LANES, column.shape[1]))
                square = jnp.dot(rowmat[at, :], column[:, part], preferred_element_type=f32)
                for b in range(own_blocks):
                    value = jnp.maximum(square[b * BLK:(b + 1) * BLK], 1e-30)
                    falloff = jnp.maximum(1.0 - value * lax.rsqrt(value), 0.0)
                    power = falloff * falloff
                    weight = weights[pl.ds(t * own_blocks + b, 1), part]
                    target[pl.ds(pl.multiple_of(t * tile + b * BLK, BLK), BLK), part] = (
                        power * power * (5.0 * weight - (4.0 * weight) * falloff)).astype(bf)
            return carry
        lax.fori_loop(0, part_blocks // own_blocks, step, 0)

    nc = {}

    def forward(u):
        for copy in zc[u]:
            copy.wait_recv()
        for v in AHEAD.get(u, ()):
            if v < count:
                for copy in zc[v]:
                    copy.start()
        nc[u] = []
        for s in range(1, nodes):
            q = lax.rem(me_n + s, nodes)
            for k in range(SEND):
                stages[u][s * SEND + k] = zs[u][chosen(q, k)]
            copy = pltpu.make_async_remote_copy(
                stages[u].at[pl.ds(s * SEND, SEND)],
                fars[u].at[pl.ds((nodes - 1 - s) * SEND, SEND)],
                n_send.at[u * nodes + s], n_recv.at[u * nodes + s],
                device_id={"node": q}, device_id_type=MESH)
            copy.start()
            nc[u].append(copy)

    def add(terms, c0, cw, first=False, last=False):
        for is_far, u in terms:
            if is_far:
                for copy in nc[u]:
                    copy.wait_recv()

        def step(r, carry):
            at = pl.ds(pl.multiple_of(r * 2 * tile, 2 * tile), 2 * tile)
            total = None if first else partial[at, c0:c0 + cw]
            for is_far, u in terms:
                a, p0, pw = spans[u]
                source = (fars if is_far else zs)[u]
                kern = far_kern if is_far else near_kern
                deep = source.shape[0] * TALL
                start = a // TALL * deep
                term = jnp.dot(
                    kern[at, start:start + deep], source[:, :, c0 - p0:c0 - p0 + cw].reshape(deep, cw),
                    preferred_element_type=f32)
                total = term if total is None else total + term
            if last:
                scale = jnp.concatenate([amps[at, :]] * (cw // LANES), axis=1)
                out[at, c0:c0 + cw] = (total * scale).astype(bf)
            else:
                partial[at, c0:c0 + cw] = total
            return carry
        lax.fori_loop(0, part_blocks // own_blocks // 2, step, 0)

    lax.fori_loop(0, part_blocks, row_step, 0)
    prepare(False)
    build(False)
    forward(0)
    for copy in gn:
        copy.wait_recv()
    prepare(True)
    build(True)
    add([(False, 0)], 0, width, first=True)
    forward(1)
    add([(False, 1), (True, 0)], 0, width)
    forward(2)
    add([(False, 2), (True, 1)], 0, width)
    forward(3)
    add([(False, 3)], *spans[3][1:])
    for u in range(4, count):
        forward(u)
        add([(False, u)], *spans[u][1:])
    add([(True, 2)], 0, width)
    for u in range(3, count):
        add([(True, u)], *spans[u][1:], last=True)

    for copy in gz + gn:
        copy.wait_send()
    for u in range(count):
        for copy in zc[u] + nc[u]:
            copy.wait_send()


def on_device(field, node_geometry, taps, boundary, sends, cols):
    tm = lax.axis_size("tm")
    nodes = lax.axis_size("node")
    rows, steps = field.shape
    part_blocks, nnz = cols.shape
    nloc = nnz - 4
    if part_blocks > nloc:
        return wide_on_device(field, node_geometry, taps, boundary, sends, cols)
    own_blocks = rows // BLK
    width = steps // tm
    sizes = (tm, nodes, width, part_blocks, nnz, nloc, own_blocks)
    spans = plan(width)
    groups = range(0, BLK, TALL)
    count = len(spans)
    slab = part_blocks * BLK
    slots = (nodes - 1) * SEND
    bf, f32 = jnp.bfloat16, jnp.float32
    dma = pltpu.SemaphoreType.DMA
    return pl.pallas_call(
        functools.partial(body, sizes),
        out_shape=pltpu.VMEM((slab, width), bf),
        in_specs=[pl.BlockSpec(memory_space=pl.ANY)] * 6,
        out_specs=pl.BlockSpec(memory_space=pltpu.VMEM),
        scratch_shapes=[
            pltpu.VMEM(node_geometry.shape, f32),
            pltpu.VMEM(taps.shape, bf),
            pltpu.SMEM(boundary.shape, jnp.int32),
            pltpu.SMEM(sends.shape, jnp.int32),
            pltpu.VMEM(cols.shape, jnp.int32),
            pltpu.VMEM((own_blocks, BLK, steps + 2 * LANES), bf),
            pltpu.VMEM((WIN + 2 * LANES, WIN), bf),
            pltpu.VMEM((slab, width), f32),
            pltpu.VMEM((slab, LANES), f32),
            pltpu.VMEM((part_blocks, 8, BLK), f32),
            pltpu.VMEM((nodes * SEND, 8, BLK), f32),
            pltpu.VMEM((slots, 8, BLK), f32),
            pltpu.VMEM((slab, 48), bf),
            *[pltpu.VMEM((tm - 1, own_blocks, TALL, cw), bf) for _, _, cw in spans],
            *[pltpu.VMEM((part_blocks, TALL, cw), bf) for _, _, cw in spans],
            *[pltpu.VMEM((nodes * SEND, TALL, cw), bf) for _, _, cw in spans],
            *[pltpu.VMEM((slots, TALL, cw), bf) for _, _, cw in spans],
            pltpu.VMEM((slab, slab), bf), pltpu.VMEM((slab, slots * BLK), bf),
            pltpu.VMEM((48, slab), bf), pltpu.VMEM((48, slots * BLK), bf),
            pltpu.VMEM((part_blocks, slab), f32), pltpu.VMEM((part_blocks, slots * BLK), f32),
            dma((5,)), dma((len(groups),)),
            dma((tm,)), dma((tm,)),
            dma((nodes,)), dma((nodes,)),
            dma((count * tm,)), dma((count * tm,)),
            dma((count * nodes,)), dma((count * nodes,)),
        ],
        compiler_params=pltpu.CompilerParams(
            collective_id=0, has_side_effects=True, vmem_limit_bytes=58 * 1024 * 1024
        ),
    )(field.reshape(own_blocks, BLK, steps), node_geometry, taps, boundary, sends, cols)


def solution(mesh):
    return jax.shard_map(
        on_device,
        mesh=mesh,
        in_specs=(
            P(("parts", "node", "tm"), None),
            P(None, ("node", "tm")),
            P(),
            P("node", None),
            P(),
            P("node", None),
        ),
        out_specs=P(("parts", "node"), "tm"),
        check_vma=False,
    )
```

```python
import functools
import math

import jax
import jax.numpy as jnp
from jax import lax
from jax.experimental import pallas as pl
from jax.experimental.pallas import tpu as pltpu
from jax.sharding import PartitionSpec as P

BLK = 128
SEND = 4
LANES = 128
MESH = pl.DeviceIdType.MESH
SUPPORT_RADIUS = 0.2


def wide_pieces(chunks):
    counts = ([1] * chunks + [1, 1, 2, 4])[-chunks:] if chunks <= 4 else [1] * (chunks - 2) + [2, 4]
    return [(c, h, counts[c]) for c in range(chunks) for h in range(counts[c])]


def wide_body(
    sizes, field, geo, taps, boundary, sends, cols, out,
    padded, table, partial, filt, geo_own, geo_stage, geo_far, kern, *rest,
):
    tm, nodes, chunks, part_blocks, nnz, nloc, own_blocks = sizes
    rest = list(rest)
    parts = wide_pieces(chunks)
    zs = [rest.pop(0) for _ in parts]
    stages = [rest.pop(0) for _ in parts]
    fars = [rest.pop(0) for _ in parts]
    outs = [rest.pop(0) for _ in range(chunks)]
    (load_sem, own_sem, out_sem, gz_send, gz_recv, gn_send, gn_recv,
     z_send, z_recv, n_send, n_recv) = rest
    me_t = lax.axis_index("tm")
    me_n = lax.axis_index("node")
    rows = own_blocks * BLK
    steps = tm * chunks * LANES

    load = pltpu.make_async_copy(field, padded.at[:, pl.ds(LANES, steps)], load_sem)
    load.start()

    barrier = pltpu.get_barrier_semaphore()
    for s in range(1, tm):
        pl.semaphore_signal(barrier, inc=1, device_id={"tm": lax.rem(me_t + s, tm)}, device_id_type=MESH)
    for s in range(1, nodes):
        pl.semaphore_signal(barrier, inc=1, device_id={"node": lax.rem(me_n + s, nodes)}, device_id_type=MESH)

    padded[:, :LANES] = jnp.zeros((rows, LANES), padded.dtype)
    padded[:, LANES + steps:] = jnp.zeros((rows, LANES), padded.dtype)
    for b in range(own_blocks):
        geo_own[pl.ds(me_t * own_blocks + b, 1), 0:4, :] = geo[:, b * BLK:(b + 1) * BLK][None]
    ntaps = taps.shape[0]
    half = (ntaps - 1) // 2
    top = LANES - half
    span = LANES + 2 * half
    lag = (
        lax.broadcasted_iota(jnp.int32, (span, LANES), 0)
        - lax.broadcasted_iota(jnp.int32, (span, LANES), 1)
    )
    table[:top, :] = jnp.zeros((top, LANES), table.dtype)
    table[top + span:, :] = jnp.zeros((top, LANES), table.dtype)
    table[top:top + span, :] = lax.fori_loop(
        0, ntaps, lambda d, acc: jnp.where(lag == d, taps[d], acc),
        jnp.zeros((span, LANES), jnp.float32),
    ).astype(table.dtype)
    pl.semaphore_wait(barrier, tm + nodes - 2)

    my_geo = geo_own.at[pl.ds(me_t * own_blocks, own_blocks)]
    gz = [
        pltpu.make_async_remote_copy(
            my_geo, my_geo, gz_send.at[s], gz_recv.at[s],
            device_id={"tm": lax.rem(me_t + s, tm)}, device_id_type=MESH)
        for s in range(1, tm)
    ]
    for copy in gz:
        copy.start()
    load.wait()

    order = sorted(range(1, tm), key=lambda s: abs(s - tm / 2))
    zc = []
    for c in range(chunks):
        for s in order + [0]:
            dest = lax.rem(me_t + s, tm)
            at = pl.multiple_of((dest * chunks + c) * LANES, LANES)
            value = jnp.dot(
                padded[:, pl.ds(at, 3 * LANES)], table[...], preferred_element_type=jnp.float32
            ).astype(jnp.bfloat16).reshape(own_blocks, BLK, LANES)
            filt[c * tm + s] = value
        for u, (_, h, count) in enumerate(parts):
            if parts[u][0] != c:
                continue
            height = BLK // count
            mine = pl.ds(me_t * own_blocks, own_blocks)
            for s in order:
                copy = pltpu.make_async_remote_copy(
                    filt.at[c * tm + s, :, pl.ds(h * height, height)],
                    zs[u].at[mine],
                    z_send.at[u * tm + s], z_recv.at[u * tm + s],
                    device_id={"tm": lax.rem(me_t + s, tm)}, device_id_type=MESH)
                if u < 2:
                    copy.start()
                zc.append((u, copy))
            zs[u][mine] = filt[c * tm, :, h * height:(h + 1) * height, :]

    def chosen(q, k):
        return boundary[0, sends[me_n, q, k]]

    for copy in gz:
        copy.wait_recv()
    gn = []
    for s in range(1, nodes):
        q = lax.rem(me_n + s, nodes)
        for k in range(SEND):
            geo_stage[s * SEND + k] = geo_own[chosen(q, k)]
        copy = pltpu.make_async_remote_copy(
            geo_stage.at[pl.ds(s * SEND, SEND)],
            geo_far.at[pl.ds((nodes - 1 - s) * SEND, SEND)],
            gn_send.at[s], gn_recv.at[s],
            device_id={"node": q}, device_id_type=MESH)
        copy.start()
        gn.append(copy)

    slots = (nodes - 1) * SEND
    dense = part_blocks <= nloc

    def far_slot(value):
        at = jnp.maximum(value - part_blocks, 0)
        src = lax.rem(at // SEND + nodes - 1 - me_n, nodes)
        return jnp.minimum(src * SEND + lax.rem(at, SEND), slots - 1)

    def build(lo, hi):
        def step(r, carry):
            mine = geo_own[r]
            spread = [
                jnp.transpose(jnp.broadcast_to(mine[axis:axis + 1], (BLK, BLK)))
                for axis in range(4)
            ]
            row = [v * (1.0 / SUPPORT_RADIUS) for v in spread[:3]]
            amp = spread[3] * (1.0 / math.sqrt(nnz))
            for g in range(lo, hi):
                if dense:
                    if g < part_blocks:
                        other, name, among = geo_own[g], g, range(nloc)
                    else:
                        rel, slot = divmod(g - part_blocks, SEND)
                        other, among = geo_far[g - part_blocks], range(nloc, nnz)
                        name = part_blocks + lax.rem(me_n + 1 + rel, nodes) * SEND + slot
                    count = 0
                    for k in among:
                        count = count + (cols[r, k] == name).astype(jnp.int32)
                    weight = other[3:4] * count.astype(jnp.float32)
                else:
                    if g < nloc:
                        other = geo_own[cols[r, g]]
                    else:
                        other = geo_far[far_slot(cols[r, g])]
                    weight = other[3:4]
                total = None
                for axis in range(3):
                    diff = row[axis] - other[axis:axis + 1] * (1.0 / SUPPORT_RADIUS)
                    total = diff * diff if total is None else total + diff * diff
                scaled = total * lax.rsqrt(jnp.maximum(total, 1e-30))
                falloff = jnp.maximum(1.0 - scaled, 0.0)
                square = falloff * falloff
                values = square * square * (4.0 * scaled + 1.0)
                kern[r, :, g * BLK:(g + 1) * BLK] = (amp * weight * values).astype(jnp.bfloat16)
            return carry
        lax.fori_loop(0, part_blocks, step, 0)

    nc = []

    ahead = {u: (u + 2,) for u in range(len(parts))}
    if len(parts) == 8:
        ahead = {0: (2, 3), 1: (4, 5), 2: (6,), 3: (7,)}

    def forward(u):
        for at, copy in zc:
            if at == u:
                copy.wait_recv()
        for at, copy in zc:
            if at in ahead.get(u, ()):
                copy.start()
        for s in range(1, nodes):
            q = lax.rem(me_n + s, nodes)
            for k in range(SEND):
                stages[u][s * SEND + k] = zs[u][chosen(q, k)]
            copy = pltpu.make_async_remote_copy(
                stages[u].at[pl.ds(s * SEND, SEND)],
                fars[u].at[pl.ds((nodes - 1 - s) * SEND, SEND)],
                n_send.at[u * nodes + s], n_recv.at[u * nodes + s],
                device_id={"node": q}, device_id_type=MESH)
            copy.start()
            nc.append((u, copy))

    outc = []

    split = part_blocks if dense else nloc
    width = part_blocks + slots if dense else nnz
    tile = own_blocks if dense else 1

    def of(c):
        return [u for u, piece in enumerate(parts) if piece[0] == c]

    def product(r, c, lo, hi):
        if dense:
            source = zs if lo == 0 else fars
            right = jnp.concatenate(
                [source[u][...] for u in of(c)], axis=1
            ).reshape((hi - lo) * BLK, LANES)
        else:
            right = jnp.concatenate([
                zs[u][cols[r, k]] if k < nloc else fars[u][far_slot(cols[r, k])]
                for k in range(lo, hi) for u in of(c)
            ], axis=0)
        left = kern[pl.ds(r * tile, tile), :, lo * BLK:hi * BLK]
        return jnp.dot(
            left.reshape(tile * BLK, (hi - lo) * BLK), right,
            preferred_element_type=jnp.float32)

    def local(c):
        def step(r, carry):
            partial[pl.ds(r * tile, tile)] = product(r, c, 0, split).reshape(tile, BLK, LANES)
            return carry
        lax.fori_loop(0, part_blocks // tile, step, 0)

    def far(c):
        for at, copy in nc:
            if parts[at][0] == c:
                copy.wait_recv()

        def step(r, carry):
            total = partial[pl.ds(r * tile, tile)].reshape(tile * BLK, LANES) + product(r, c, split, width)
            outs[c][pl.ds(pl.multiple_of(r * tile * BLK, tile * BLK), tile * BLK), :] = total.astype(jnp.bfloat16)
            return carry
        lax.fori_loop(0, part_blocks // tile, step, 0)
        copy = pltpu.make_async_copy(outs[c], out.at[:, pl.ds(c * LANES, LANES)], out_sem.at[c])
        copy.start()
        outc.append(copy)

    build(0, split)
    for u in of(0)[:1]:
        forward(u)
    for copy in gn:
        copy.wait_recv()
    build(split, width)
    for u in of(0)[1:]:
        forward(u)
    local(0)
    for c in range(1, chunks):
        todo = of(c)
        for u in todo[:-1] if len(todo) > 2 else todo[:1]:
            forward(u)
        far(c - 1)
        for u in todo[-1:] if len(todo) > 1 else []:
            forward(u)
        local(c)
    far(chunks - 1)

    for copy in gz + gn:
        copy.wait_send()
    for _, copy in zc + nc:
        copy.wait_send()
    for copy in outc:
        copy.wait()


def wide_on_device(field, node_geometry, taps, boundary, sends, cols):
    tm = lax.axis_size("tm")
    nodes = lax.axis_size("node")
    rows, steps = field.shape
    part_blocks, nnz = cols.shape
    nloc = nnz - 4
    own_blocks = rows // BLK
    chunks = steps // tm // LANES
    parts = wide_pieces(chunks)
    sizes = (tm, nodes, chunks, part_blocks, nnz, nloc, own_blocks)
    slab = part_blocks * BLK
    slots = (nodes - 1) * SEND
    width = part_blocks + slots if part_blocks <= nloc else nnz
    bf = jnp.bfloat16
    dma = pltpu.SemaphoreType.DMA
    return pl.pallas_call(
        functools.partial(wide_body, sizes),
        out_shape=pltpu.VMEM((slab, steps // tm), bf),
        in_specs=[
            pl.BlockSpec(memory_space=pl.ANY),
            pl.BlockSpec(memory_space=pltpu.VMEM),
            pl.BlockSpec(memory_space=pltpu.SMEM),
            pl.BlockSpec(memory_space=pltpu.SMEM),
            pl.BlockSpec(memory_space=pltpu.SMEM),
            pl.BlockSpec(memory_space=pltpu.SMEM),
        ],
        out_specs=pl.BlockSpec(memory_space=pltpu.VMEM),
        scratch_shapes=[
            pltpu.VMEM((rows, steps + 2 * LANES), bf),
            pltpu.VMEM((3 * LANES, LANES), bf),
            pltpu.VMEM((part_blocks, BLK, LANES), jnp.float32),
            pltpu.VMEM((chunks * tm, own_blocks, BLK, LANES), bf),
            pltpu.VMEM((part_blocks, 8, BLK), jnp.float32),
            pltpu.VMEM((nodes * SEND, 8, BLK), jnp.float32),
            pltpu.VMEM((slots, 8, BLK), jnp.float32),
            pltpu.VMEM((part_blocks, BLK, width * BLK), bf),
            *[pltpu.VMEM((part_blocks, BLK // p[2], LANES), bf) for p in parts],
            *[pltpu.VMEM((nodes * SEND, BLK // p[2], LANES), bf) for p in parts],
            *[pltpu.VMEM((slots, BLK // p[2], LANES), bf) for p in parts],
            *[pltpu.VMEM((slab, LANES), bf) for _ in range(chunks)],
            dma, dma,
            dma((chunks,)),
            dma((tm,)), dma((tm,)),
            dma((nodes,)), dma((nodes,)),
            dma((len(parts) * tm,)), dma((len(parts) * tm,)),
            dma((len(parts) * nodes,)), dma((len(parts) * nodes,)),
        ],
        compiler_params=pltpu.CompilerParams(
            collective_id=0, has_side_effects=True, vmem_limit_bytes=58 * 1024 * 1024
        ),
    )(field, node_geometry, taps.astype(jnp.float32), boundary, sends, cols)


WIN = 256


TALL = 32


def plan(width):
    parts = [(0, 0, 2), (0, 2, 2), (1, 0, 2), (1, 2, 2), (2, 0, 2), (2, 2, 2), (3, 0, 2), (3, 2, 1), (3, 3, 1)]
    unit = width // 4
    spans = [(group * TALL, at * unit, wide * unit) for group, at, wide in parts]
    return spans


WINDOW = 4


def ahead(spans):
    unit = spans[-1][2]
    order, flying, at = [], 0, 0
    for u in range(-1, len(spans)):
        if u >= 0:
            flying -= spans[u][2]
        starts = []
        while at < len(spans) and (flying == 0 or flying + spans[at][2] <= WINDOW * unit):
            starts.append(at)
            flying += spans[at][2]
            at += 1
        order.append(starts)
    return order


def body(
    sizes, field, geo_in, taps_in, boundary_in, sends_in, cols_in, out,
    geo, taps, boundary, sends, cols, padded, table, partial, amps, geo_own, geo_stage, geo_far, rowmat, *rest,
):
    tm, nodes, width, part_blocks, nnz, nloc, own_blocks = sizes
    spans = plan(width)
    groups = range(0, BLK, TALL)
    count = len(spans)
    starts = ahead(spans)
    rest = list(rest)
    filts = [rest.pop(0) for _ in spans]
    zs = [rest.pop(0) for _ in spans]
    stages = [rest.pop(0) for _ in spans]
    fars = [rest.pop(0) for _ in spans]
    (near_kern, far_kern, near_cols, far_cols, near_weight, far_weight, small_sem, load_sem, gz_send, gz_recv, gn_send, gn_recv, z_send, z_recv, n_send, n_recv) = rest
    me_t = lax.axis_index("tm")
    me_n = lax.axis_index("node")
    steps = tm * width
    slots = (nodes - 1) * SEND
    f32, bf = jnp.float32, jnp.bfloat16

    barrier = pltpu.get_barrier_semaphore()
    for s in range(1, tm):
        pl.semaphore_signal(barrier, inc=1, device_id={"tm": lax.rem(me_t + s, tm)}, device_id_type=MESH)
    for s in range(1, nodes):
        pl.semaphore_signal(barrier, inc=1, device_id={"node": lax.rem(me_n + s, nodes)}, device_id_type=MESH)

    small = [
        pltpu.make_async_copy(source, target, small_sem.at[i])
        for i, (source, target) in enumerate((
            (taps_in, taps), (geo_in, geo), (boundary_in, boundary), (sends_in, sends), (cols_in, cols)))
    ]
    for copy in small[:1]:
        copy.start()
    loads = {}
    for i, a in enumerate(groups):
        loads[a] = pltpu.make_async_copy(
            field.at[:, pl.ds(a, TALL)], padded.at[:, pl.ds(a, TALL), pl.ds(LANES, steps)], load_sem.at[i])
        loads[a].start()
    for copy in small[1:]:
        copy.start()

    padded[:, :, :LANES] = jnp.zeros((own_blocks, BLK, LANES), bf)
    padded[:, :, LANES + steps:] = jnp.zeros((own_blocks, BLK, LANES), bf)
    table[...] = jnp.zeros(table.shape, bf)
    small[0].wait()
    small[1].wait()
    for b in range(own_blocks):
        geo_own[pl.ds(me_t * own_blocks + b, 1), 0:4, :] = geo[:, b * BLK:(b + 1) * BLK][None]

    ntaps = taps.shape[0]
    half = (ntaps - 1) // 2
    top = LANES - half
    line = jnp.concatenate(
        [taps[...].astype(f32).reshape(1, ntaps), jnp.zeros((1, 2 * LANES - ntaps), f32)], axis=1)
    slanted = pltpu.roll(jnp.broadcast_to(line, (LANES, 2 * LANES)), 0, 1, stride=1, stride_axis=0)
    toeplitz = jnp.transpose(slanted).astype(bf)
    for w in range(WIN // LANES):
        table[top + w * LANES:top + (w + 2) * LANES, w * LANES:(w + 1) * LANES] = toeplitz

    order = sorted(range(1, tm), key=lambda s: abs(s - tm / 2))
    zc = {}

    def partner(s):
        return lax.rem(me_t + s, tm)

    mine = pl.ds(me_t * own_blocks, own_blocks)

    def filtering(u):
        a, c0, cw = spans[u]
        for s in order + [0]:
            dest = partner(s)
            for w in range(0, cw, WIN):
                n = min(WIN, cw - w)
                at = pl.multiple_of(dest * width + c0 + w, LANES)
                window = padded[:, a:a + TALL, pl.ds(at, n + 2 * LANES)].reshape(own_blocks * TALL, n + 2 * LANES)
                value = jnp.dot(window, table[:n + 2 * LANES, :n], preferred_element_type=f32)
                value = value.astype(bf).reshape(own_blocks, TALL, n)
                if s:
                    filts[u][s - 1, :, :, w:w + n] = value
                else:
                    zs[u][mine, :, w:w + n] = value
        zc[u] = [
            pltpu.make_async_remote_copy(
                filts[u].at[s - 1], zs[u].at[mine],
                z_send.at[u * tm + s], z_recv.at[u * tm + s],
                device_id={"tm": partner(s)}, device_id_type=MESH)
            for s in order
        ]

    for u in range(1):
        loads[spans[u][0]].wait()
        filtering(u)
    pl.semaphore_wait(barrier, tm + nodes - 2)
    my_geo = geo_own.at[mine, pl.ds(0, 4)]
    gz = [
        pltpu.make_async_remote_copy(
            my_geo, my_geo, gz_send.at[s], gz_recv.at[s],
            device_id={"tm": partner(s)}, device_id_type=MESH)
        for s in order
    ]
    for copy in gz:
        copy.start()
    for copy in zc[0]:
        copy.start()
    waited = {spans[0][0]}
    for u in range(1, count):
        if spans[u][0] not in waited:
            loads[spans[u][0]].wait()
            waited.add(spans[u][0])
        filtering(u)
        if u in starts[0]:
            for copy in zc[u]:
                copy.start()

    for copy in small[2:]:
        copy.wait()

    def chosen(q, k):
        return boundary[0, sends[me_n, q, k]]

    for copy in gz:
        copy.wait_recv()
    gn = []
    for s in range(1, nodes):
        q = lax.rem(me_n + s, nodes)
        for k in range(SEND):
            geo_stage[s * SEND + k] = geo_own[chosen(q, k)]
        copy = pltpu.make_async_remote_copy(
            geo_stage.at[pl.ds(s * SEND, SEND)],
            geo_far.at[pl.ds((nodes - 1 - s) * SEND, SEND)],
            gn_send.at[s], gn_recv.at[s],
            device_id={"node": q}, device_id_type=MESH)
        copy.start()
        gn.append(copy)

    tile = own_blocks * BLK

    def halves(value):
        high = value.astype(bf).astype(f32)
        rest = value - high
        middle = rest.astype(bf).astype(f32)
        return high, middle, rest - middle

    def scaled(block):
        row = lax.broadcasted_iota(jnp.int32, block.shape, 0)
        point = jnp.where(row < 3, (block - 0.5) * (1.0 / SUPPORT_RADIUS), 0.0)
        norm = jnp.broadcast_to(jnp.sum(point * point, axis=0, keepdims=True), block.shape)
        return row, point, norm

    def left(block):
        row, point, norm = scaled(block)
        high, middle, low = halves(jnp.where(row < 3, -2.0 * point, jnp.where(row == 3, norm, jnp.where(row == 4, 1.0, 0.0))))
        return jnp.concatenate([high, high, middle, middle, high, low], axis=0)

    def right(block):
        row, point, norm = scaled(block)
        high, middle, low = halves(jnp.where(row < 3, point, jnp.where(row == 3, 1.0, jnp.where(row == 4, norm, 0.0))))
        return jnp.concatenate([high, middle, high, middle, low, high], axis=0)

    def row_step(r, carry):
        block = geo_own[r]
        at = pl.ds(pl.multiple_of(r * BLK, BLK), BLK)
        rowmat[at, :] = jnp.transpose(left(block)).astype(bf)
        amps[at, :] = jnp.transpose(jnp.broadcast_to(block[3:4] * (1.0 / math.sqrt(nnz)), (BLK, BLK)))
        return carry

    def prepare(is_far):
        source, blocks = (geo_far, slots) if is_far else (geo_own, part_blocks)
        joined = jnp.concatenate([source[g, :, a:a + TALL] for a in groups for g in range(blocks)], axis=1)
        (far_cols if is_far else near_cols)[...] = right(joined).astype(bf)
        lane = lax.broadcasted_iota(jnp.int32, (part_blocks, blocks * TALL), 1)
        name = lax.shift_right_logical(lane, TALL.bit_length() - 1)
        if is_far:
            owner = me_n + 1 + lax.shift_right_logical(name, 2)
            owner = jnp.where(owner >= nodes, owner - nodes, owner)
            name = part_blocks + owner * SEND + jnp.bitwise_and(name, SEND - 1)
        total = jnp.zeros(name.shape, f32)
        for k in range(nloc, nnz) if is_far else range(nloc):
            total = total + jnp.where(cols[:, k:k + 1] == name, 1.0, 0.0)
        total = jnp.concatenate([total] * len(groups), axis=1)
        (far_weight if is_far else near_weight)[...] = total * joined[3:4]

    def build(is_far):
        column = far_cols if is_far else near_cols
        weights = far_weight if is_far else near_weight
        target = far_kern if is_far else near_kern

        def step(t, carry):
            at = pl.ds(pl.multiple_of(t * tile, tile), tile)
            for lo in range(0, column.shape[1], 3 * LANES):
                part = slice(lo, min(lo + 3 * LANES, column.shape[1]))
                square = jnp.dot(rowmat[at, :], column[:, part], preferred_element_type=f32)
                for b in range(own_blocks):
                    value = jnp.maximum(square[b * BLK:(b + 1) * BLK], 1e-30)
                    falloff = jnp.maximum(1.0 - value * lax.rsqrt(value), 0.0)
                    power = falloff * falloff
                    weight = weights[pl.ds(t * own_blocks + b, 1), part]
                    target[pl.ds(pl.multiple_of(t * tile + b * BLK, BLK), BLK), part] = (
                        power * power * (5.0 * weight - (4.0 * weight) * falloff)).astype(bf)
            return carry
        lax.fori_loop(0, part_blocks // own_blocks, step, 0)

    nc, sent = {}, []

    def forward(u):
        for copy in zc[u]:
            copy.wait_recv()
        for v in starts[u + 1]:
            for copy in zc[v]:
                copy.start()
        nc[u] = []
        for s in range(1, nodes):
            q = lax.rem(me_n + s, nodes)
            for k in range(SEND):
                stages[u][s * SEND + k] = zs[u][chosen(q, k)]
            copy = pltpu.make_async_remote_copy(
                stages[u].at[pl.ds(s * SEND, SEND)],
                fars[u].at[pl.ds((nodes - 1 - s) * SEND, SEND)],
                n_send.at[u * nodes + s], n_recv.at[u * nodes + s],
                device_id={"node": q}, device_id_type=MESH)
            copy.start()
            nc[u].append(copy)
            sent.append(copy)

    def add(is_far, picked, c0, cw, first=False, last=False):
        held = [[u for u, (a, p0, pw) in enumerate(spans)
                 if a == group * TALL and p0 < c0 + cw and c0 < p0 + pw] for group in picked]
        if is_far:
            for u in sum(held, []):
                if u in nc:
                    for copy in nc.pop(u):
                        copy.wait_recv()
        refs = fars if is_far else zs
        blocks = slots if is_far else part_blocks
        deep = blocks * TALL
        kern = far_kern if is_far else near_kern

        def step(r, carry):
            at = pl.ds(pl.multiple_of(r * 2 * tile, 2 * tile), 2 * tile)
            right = jnp.concatenate([
                jnp.concatenate([
                    refs[u][:, :, max(c0 - spans[u][1], 0):min(c0 + cw - spans[u][1], spans[u][2])]
                    for u in row
                ], axis=2).reshape(deep, cw)
                for row in held
            ], axis=0)
            total = jnp.dot(
                kern[at, picked[0] * deep:(picked[-1] + 1) * deep], right, preferred_element_type=f32)
            if not first:
                total = total + partial[at, c0:c0 + cw]
            if last:
                scale = jnp.concatenate([amps[at, :]] * (cw // LANES), axis=1)
                out[at, c0:c0 + cw] = (total * scale).astype(bf)
            else:
                partial[at, c0:c0 + cw] = total
            return carry
        lax.fori_loop(0, part_blocks // own_blocks // 2, step, 0)

    def near():
        lax.fori_loop(0, part_blocks, row_step, 0, unroll=4)
        prepare(False)
        build(False)

    def far():
        for copy in gn:
            copy.wait_recv()
        prepare(True)
        build(True)

    forward(0)
    near()
    forward(1)
    far()
    forward(2)
    forward(3)
    add(False, [0, 1], 0, width, first=True)
    forward(4)
    add(True, [0, 1], 0, width)
    forward(5)
    add(False, [2], 0, width)
    forward(6)
    add(True, [2], 0, width)
    forward(7)
    forward(8)
    add(False, [3], 0, width)
    add(True, [3], *spans[6][1:], last=True)
    add(True, [3], *spans[7][1:], last=True)
    add(True, [3], *spans[8][1:], last=True)

    for copy in gz + gn:
        copy.wait_send()
    for u in range(count):
        for copy in zc[u]:
            copy.wait_send()
    for copy in sent:
        copy.wait_send()


def on_device(field, node_geometry, taps, boundary, sends, cols):
    tm = lax.axis_size("tm")
    nodes = lax.axis_size("node")
    rows, steps = field.shape
    part_blocks, nnz = cols.shape
    nloc = nnz - 4
    if part_blocks > nloc:
        return wide_on_device(field, node_geometry, taps, boundary, sends, cols)
    own_blocks = rows // BLK
    width = steps // tm
    sizes = (tm, nodes, width, part_blocks, nnz, nloc, own_blocks)
    spans = plan(width)
    groups = range(0, BLK, TALL)
    count = len(spans)
    slab = part_blocks * BLK
    slots = (nodes - 1) * SEND
    bf, f32 = jnp.bfloat16, jnp.float32
    dma = pltpu.SemaphoreType.DMA
    return pl.pallas_call(
        functools.partial(body, sizes),
        out_shape=pltpu.VMEM((slab, width), bf),
        in_specs=[pl.BlockSpec(memory_space=pl.ANY)] * 6,
        out_specs=pl.BlockSpec(memory_space=pltpu.VMEM),
        scratch_shapes=[
            pltpu.VMEM(node_geometry.shape, f32),
            pltpu.VMEM(taps.shape, bf),
            pltpu.SMEM(boundary.shape, jnp.int32),
            pltpu.SMEM(sends.shape, jnp.int32),
            pltpu.VMEM(cols.shape, jnp.int32),
            pltpu.VMEM((own_blocks, BLK, steps + 2 * LANES), bf),
            pltpu.VMEM((WIN + 2 * LANES, WIN), bf),
            pltpu.VMEM((slab, width), f32),
            pltpu.VMEM((slab, LANES), f32),
            pltpu.VMEM((part_blocks, 8, BLK), f32),
            pltpu.VMEM((nodes * SEND, 8, BLK), f32),
            pltpu.VMEM((slots, 8, BLK), f32),
            pltpu.VMEM((slab, 48), bf),
            *[pltpu.VMEM((tm - 1, own_blocks, TALL, cw), bf) for _, _, cw in spans],
            *[pltpu.VMEM((part_blocks, TALL, cw), bf) for _, _, cw in spans],
            *[pltpu.VMEM((nodes * SEND, TALL, cw), bf) for _, _, cw in spans],
            *[pltpu.VMEM((slots, TALL, cw), bf) for _, _, cw in spans],
            pltpu.VMEM((slab, slab), bf), pltpu.VMEM((slab, slots * BLK), bf),
            pltpu.VMEM((48, slab), bf), pltpu.VMEM((48, slots * BLK), bf),
            pltpu.VMEM((part_blocks, slab), f32), pltpu.VMEM((part_blocks, slots * BLK), f32),
            dma((5,)), dma((len(groups),)),
            dma((tm,)), dma((tm,)),
            dma((nodes,)), dma((nodes,)),
            dma((count * tm,)), dma((count * tm,)),
            dma((count * nodes,)), dma((count * nodes,)),
        ],
        compiler_params=pltpu.CompilerParams(
            collective_id=0, has_side_effects=True, vmem_limit_bytes=58 * 1024 * 1024
        ),
    )(field.reshape(own_blocks, BLK, steps), node_geometry, taps, boundary, sends, cols)


def solution(mesh):
    return jax.shard_map(
        on_device,
        mesh=mesh,
        in_specs=(
            P(("parts", "node", "tm"), None),
            P(None, ("node", "tm")),
            P(),
            P("node", None),
            P(),
            P("node", None),
        ),
        out_specs=P(("parts", "node"), "tm"),
        check_vma=False,
    )
```

```python
import functools
import math

import jax
import jax.numpy as jnp
from jax import lax
from jax.experimental import pallas as pl
from jax.experimental.pallas import tpu as pltpu
from jax.sharding import PartitionSpec as P

BLK = 128
SEND = 4
LANES = 128
MESH = pl.DeviceIdType.MESH
SUPPORT_RADIUS = 0.2


def wide_pieces(chunks):
    counts = ([1] * chunks + [1, 1, 2, 4])[-chunks:] if chunks <= 4 else [1] * (chunks - 2) + [2, 4]
    return [(c, h, counts[c]) for c in range(chunks) for h in range(counts[c])]


def wide_body(
    sizes, field, geo, taps, boundary, sends, cols, out,
    padded, table, partial, filt, geo_own, geo_stage, geo_far, kern, *rest,
):
    tm, nodes, chunks, part_blocks, nnz, nloc, own_blocks = sizes
    rest = list(rest)
    parts = wide_pieces(chunks)
    zs = [rest.pop(0) for _ in parts]
    stages = [rest.pop(0) for _ in parts]
    fars = [rest.pop(0) for _ in parts]
    outs = [rest.pop(0) for _ in range(chunks)]
    (load_sem, own_sem, out_sem, gz_send, gz_recv, gn_send, gn_recv,
     z_send, z_recv, n_send, n_recv) = rest
    me_t = lax.axis_index("tm")
    me_n = lax.axis_index("node")
    rows = own_blocks * BLK
    steps = tm * chunks * LANES

    load = pltpu.make_async_copy(field, padded.at[:, pl.ds(LANES, steps)], load_sem)
    load.start()

    barrier = pltpu.get_barrier_semaphore()
    for s in range(1, tm):
        pl.semaphore_signal(barrier, inc=1, device_id={"tm": lax.rem(me_t + s, tm)}, device_id_type=MESH)
    for s in range(1, nodes):
        pl.semaphore_signal(barrier, inc=1, device_id={"node": lax.rem(me_n + s, nodes)}, device_id_type=MESH)

    padded[:, :LANES] = jnp.zeros((rows, LANES), padded.dtype)
    padded[:, LANES + steps:] = jnp.zeros((rows, LANES), padded.dtype)
    for b in range(own_blocks):
        geo_own[pl.ds(me_t * own_blocks + b, 1), 0:4, :] = geo[:, b * BLK:(b + 1) * BLK][None]
    ntaps = taps.shape[0]
    half = (ntaps - 1) // 2
    top = LANES - half
    span = LANES + 2 * half
    lag = (
        lax.broadcasted_iota(jnp.int32, (span, LANES), 0)
        - lax.broadcasted_iota(jnp.int32, (span, LANES), 1)
    )
    table[:top, :] = jnp.zeros((top, LANES), table.dtype)
    table[top + span:, :] = jnp.zeros((top, LANES), table.dtype)
    table[top:top + span, :] = lax.fori_loop(
        0, ntaps, lambda d, acc: jnp.where(lag == d, taps[d], acc),
        jnp.zeros((span, LANES), jnp.float32),
    ).astype(table.dtype)
    pl.semaphore_wait(barrier, tm + nodes - 2)

    my_geo = geo_own.at[pl.ds(me_t * own_blocks, own_blocks)]
    gz = [
        pltpu.make_async_remote_copy(
            my_geo, my_geo, gz_send.at[s], gz_recv.at[s],
            device_id={"tm": lax.rem(me_t + s, tm)}, device_id_type=MESH)
        for s in range(1, tm)
    ]
    for copy in gz:
        copy.start()
    load.wait()

    order = sorted(range(1, tm), key=lambda s: abs(s - tm / 2))
    zc = []
    for c in range(chunks):
        for s in order + [0]:
            dest = lax.rem(me_t + s, tm)
            at = pl.multiple_of((dest * chunks + c) * LANES, LANES)
            value = jnp.dot(
                padded[:, pl.ds(at, 3 * LANES)], table[...], preferred_element_type=jnp.float32
            ).astype(jnp.bfloat16).reshape(own_blocks, BLK, LANES)
            filt[c * tm + s] = value
        for u, (_, h, count) in enumerate(parts):
            if parts[u][0] != c:
                continue
            height = BLK // count
            mine = pl.ds(me_t * own_blocks, own_blocks)
            for s in order:
                copy = pltpu.make_async_remote_copy(
                    filt.at[c * tm + s, :, pl.ds(h * height, height)],
                    zs[u].at[mine],
                    z_send.at[u * tm + s], z_recv.at[u * tm + s],
                    device_id={"tm": lax.rem(me_t + s, tm)}, device_id_type=MESH)
                if u < 2:
                    copy.start()
                zc.append((u, copy))
            zs[u][mine] = filt[c * tm, :, h * height:(h + 1) * height, :]

    def chosen(q, k):
        return boundary[0, sends[me_n, q, k]]

    for copy in gz:
        copy.wait_recv()
    gn = []
    for s in range(1, nodes):
        q = lax.rem(me_n + s, nodes)
        for k in range(SEND):
            geo_stage[s * SEND + k] = geo_own[chosen(q, k)]
        copy = pltpu.make_async_remote_copy(
            geo_stage.at[pl.ds(s * SEND, SEND)],
            geo_far.at[pl.ds((nodes - 1 - s) * SEND, SEND)],
            gn_send.at[s], gn_recv.at[s],
            device_id={"node": q}, device_id_type=MESH)
        copy.start()
        gn.append(copy)

    slots = (nodes - 1) * SEND
    dense = part_blocks <= nloc

    def far_slot(value):
        at = jnp.maximum(value - part_blocks, 0)
        src = lax.rem(at // SEND + nodes - 1 - me_n, nodes)
        return jnp.minimum(src * SEND + lax.rem(at, SEND), slots - 1)

    def build(lo, hi):
        def step(r, carry):
            mine = geo_own[r]
            spread = [
                jnp.transpose(jnp.broadcast_to(mine[axis:axis + 1], (BLK, BLK)))
                for axis in range(4)
            ]
            row = [v * (1.0 / SUPPORT_RADIUS) for v in spread[:3]]
            amp = spread[3] * (1.0 / math.sqrt(nnz))
            for g in range(lo, hi):
                if dense:
                    if g < part_blocks:
                        other, name, among = geo_own[g], g, range(nloc)
                    else:
                        rel, slot = divmod(g - part_blocks, SEND)
                        other, among = geo_far[g - part_blocks], range(nloc, nnz)
                        name = part_blocks + lax.rem(me_n + 1 + rel, nodes) * SEND + slot
                    count = 0
                    for k in among:
                        count = count + (cols[r, k] == name).astype(jnp.int32)
                    weight = other[3:4] * count.astype(jnp.float32)
                else:
                    if g < nloc:
                        other = geo_own[cols[r, g]]
                    else:
                        other = geo_far[far_slot(cols[r, g])]
                    weight = other[3:4]
                total = None
                for axis in range(3):
                    diff = row[axis] - other[axis:axis + 1] * (1.0 / SUPPORT_RADIUS)
                    total = diff * diff if total is None else total + diff * diff
                scaled = total * lax.rsqrt(jnp.maximum(total, 1e-30))
                falloff = jnp.maximum(1.0 - scaled, 0.0)
                square = falloff * falloff
                values = square * square * (4.0 * scaled + 1.0)
                kern[r, :, g * BLK:(g + 1) * BLK] = (amp * weight * values).astype(jnp.bfloat16)
            return carry
        lax.fori_loop(0, part_blocks, step, 0)

    nc = []

    ahead = {u: (u + 2,) for u in range(len(parts))}
    if len(parts) == 8:
        ahead = {0: (2, 3), 1: (4, 5), 2: (6,), 3: (7,)}

    def forward(u):
        for at, copy in zc:
            if at == u:
                copy.wait_recv()
        for at, copy in zc:
            if at in ahead.get(u, ()):
                copy.start()
        for s in range(1, nodes):
            q = lax.rem(me_n + s, nodes)
            for k in range(SEND):
                stages[u][s * SEND + k] = zs[u][chosen(q, k)]
            copy = pltpu.make_async_remote_copy(
                stages[u].at[pl.ds(s * SEND, SEND)],
                fars[u].at[pl.ds((nodes - 1 - s) * SEND, SEND)],
                n_send.at[u * nodes + s], n_recv.at[u * nodes + s],
                device_id={"node": q}, device_id_type=MESH)
            copy.start()
            nc.append((u, copy))

    outc = []

    split = part_blocks if dense else nloc
    width = part_blocks + slots if dense else nnz
    tile = own_blocks if dense else 1

    def of(c):
        return [u for u, piece in enumerate(parts) if piece[0] == c]

    def product(r, c, lo, hi):
        if dense:
            source = zs if lo == 0 else fars
            right = jnp.concatenate(
                [source[u][...] for u in of(c)], axis=1
            ).reshape((hi - lo) * BLK, LANES)
        else:
            right = jnp.concatenate([
                zs[u][cols[r, k]] if k < nloc else fars[u][far_slot(cols[r, k])]
                for k in range(lo, hi) for u in of(c)
            ], axis=0)
        left = kern[pl.ds(r * tile, tile), :, lo * BLK:hi * BLK]
        return jnp.dot(
            left.reshape(tile * BLK, (hi - lo) * BLK), right,
            preferred_element_type=jnp.float32)

    def local(c):
        def step(r, carry):
            partial[pl.ds(r * tile, tile)] = product(r, c, 0, split).reshape(tile, BLK, LANES)
            return carry
        lax.fori_loop(0, part_blocks // tile, step, 0)

    def far(c):
        for at, copy in nc:
            if parts[at][0] == c:
                copy.wait_recv()

        def step(r, carry):
            total = partial[pl.ds(r * tile, tile)].reshape(tile * BLK, LANES) + product(r, c, split, width)
            outs[c][pl.ds(pl.multiple_of(r * tile * BLK, tile * BLK), tile * BLK), :] = total.astype(jnp.bfloat16)
            return carry
        lax.fori_loop(0, part_blocks // tile, step, 0)
        copy = pltpu.make_async_copy(outs[c], out.at[:, pl.ds(c * LANES, LANES)], out_sem.at[c])
        copy.start()
        outc.append(copy)

    build(0, split)
    for u in of(0)[:1]:
        forward(u)
    for copy in gn:
        copy.wait_recv()
    build(split, width)
    for u in of(0)[1:]:
        forward(u)
    local(0)
    for c in range(1, chunks):
        todo = of(c)
        for u in todo[:-1] if len(todo) > 2 else todo[:1]:
            forward(u)
        far(c - 1)
        for u in todo[-1:] if len(todo) > 1 else []:
            forward(u)
        local(c)
    far(chunks - 1)

    for copy in gz + gn:
        copy.wait_send()
    for _, copy in zc + nc:
        copy.wait_send()
    for copy in outc:
        copy.wait()


def wide_on_device(field, node_geometry, taps, boundary, sends, cols):
    tm = lax.axis_size("tm")
    nodes = lax.axis_size("node")
    rows, steps = field.shape
    part_blocks, nnz = cols.shape
    nloc = nnz - 4
    own_blocks = rows // BLK
    chunks = steps // tm // LANES
    parts = wide_pieces(chunks)
    sizes = (tm, nodes, chunks, part_blocks, nnz, nloc, own_blocks)
    slab = part_blocks * BLK
    slots = (nodes - 1) * SEND
    width = part_blocks + slots if part_blocks <= nloc else nnz
    bf = jnp.bfloat16
    dma = pltpu.SemaphoreType.DMA
    return pl.pallas_call(
        functools.partial(wide_body, sizes),
        out_shape=pltpu.VMEM((slab, steps // tm), bf),
        in_specs=[
            pl.BlockSpec(memory_space=pl.ANY),
            pl.BlockSpec(memory_space=pltpu.VMEM),
            pl.BlockSpec(memory_space=pltpu.SMEM),
            pl.BlockSpec(memory_space=pltpu.SMEM),
            pl.BlockSpec(memory_space=pltpu.SMEM),
            pl.BlockSpec(memory_space=pltpu.SMEM),
        ],
        out_specs=pl.BlockSpec(memory_space=pltpu.VMEM),
        scratch_shapes=[
            pltpu.VMEM((rows, steps + 2 * LANES), bf),
            pltpu.VMEM((3 * LANES, LANES), bf),
            pltpu.VMEM((part_blocks, BLK, LANES), jnp.float32),
            pltpu.VMEM((chunks * tm, own_blocks, BLK, LANES), bf),
            pltpu.VMEM((part_blocks, 8, BLK), jnp.float32),
            pltpu.VMEM((nodes * SEND, 8, BLK), jnp.float32),
            pltpu.VMEM((slots, 8, BLK), jnp.float32),
            pltpu.VMEM((part_blocks, BLK, width * BLK), bf),
            *[pltpu.VMEM((part_blocks, BLK // p[2], LANES), bf) for p in parts],
            *[pltpu.VMEM((nodes * SEND, BLK // p[2], LANES), bf) for p in parts],
            *[pltpu.VMEM((slots, BLK // p[2], LANES), bf) for p in parts],
            *[pltpu.VMEM((slab, LANES), bf) for _ in range(chunks)],
            dma, dma,
            dma((chunks,)),
            dma((tm,)), dma((tm,)),
            dma((nodes,)), dma((nodes,)),
            dma((len(parts) * tm,)), dma((len(parts) * tm,)),
            dma((len(parts) * nodes,)), dma((len(parts) * nodes,)),
        ],
        compiler_params=pltpu.CompilerParams(
            collective_id=0, has_side_effects=True, vmem_limit_bytes=58 * 1024 * 1024
        ),
    )(field, node_geometry, taps.astype(jnp.float32), boundary, sends, cols)


WIN = 256


TALL = 32


def plan(width):
    parts = [(0, 0, 2), (0, 2, 2), (1, 0, 2), (1, 2, 2), (2, 0, 2), (2, 2, 2), (3, 0, 2), (3, 2, 1), (3, 3, 1)]
    unit = width // 4
    spans = [(group * TALL, at * unit, wide * unit) for group, at, wide in parts]
    return spans


WINDOW = 4


def ahead(spans):
    unit = spans[-1][2]
    order, flying, at = [], 0, 0
    for u in range(-1, len(spans)):
        if u >= 0:
            flying -= spans[u][2]
        starts = []
        while at < len(spans) and (flying == 0 or flying + spans[at][2] <= WINDOW * unit):
            starts.append(at)
            flying += spans[at][2]
            at += 1
        order.append(starts)
    return order


def body(
    sizes, field, geo_in, taps_in, boundary_in, sends_in, cols_in, out,
    geo, taps, boundary, sends, cols, padded, table, partial, amps, geo_own, geo_stage, geo_far, rowmat, *rest,
):
    tm, nodes, width, part_blocks, nnz, nloc, own_blocks = sizes
    spans = plan(width)
    groups = range(0, BLK, TALL)
    count = len(spans)
    starts = ahead(spans)
    rest = list(rest)
    filts = [rest.pop(0) for _ in spans]
    zs = [rest.pop(0) for _ in spans]
    stages = [rest.pop(0) for _ in spans]
    fars = [rest.pop(0) for _ in spans]
    (near_kern, far_kern, near_cols, far_cols, near_weight, far_weight, small_sem, load_sem, gz_send, gz_recv, gn_send, gn_recv, z_send, z_recv, n_send, n_recv) = rest
    me_t = lax.axis_index("tm")
    me_n = lax.axis_index("node")
    inner = jnp.logical_and(me_t > 0, me_t < tm - 1)
    steps = tm * width
    slots = (nodes - 1) * SEND
    f32, bf = jnp.float32, jnp.bfloat16

    barrier = pltpu.get_barrier_semaphore()
    for s in range(1, tm):
        pl.semaphore_signal(barrier, inc=1, device_id={"tm": lax.rem(me_t + s, tm)}, device_id_type=MESH)
    for s in range(1, nodes):
        pl.semaphore_signal(barrier, inc=1, device_id={"node": lax.rem(me_n + s, nodes)}, device_id_type=MESH)

    small = [
        pltpu.make_async_copy(source, target, small_sem.at[i])
        for i, (source, target) in enumerate((
            (taps_in, taps), (geo_in, geo), (boundary_in, boundary), (sends_in, sends), (cols_in, cols)))
    ]
    for copy in small[:1]:
        copy.start()
    loads = {}
    for i, a in enumerate(groups):
        loads[a] = pltpu.make_async_copy(
            field.at[:, pl.ds(a, TALL)], padded.at[:, pl.ds(a, TALL), pl.ds(LANES, steps)], load_sem.at[i])
        loads[a].start()
    for copy in small[1:]:
        copy.start()

    padded[:, :, :LANES] = jnp.zeros((own_blocks, BLK, LANES), bf)
    padded[:, :, LANES + steps:] = jnp.zeros((own_blocks, BLK, LANES), bf)
    table[...] = jnp.zeros(table.shape, bf)
    small[0].wait()
    small[1].wait()
    for b in range(own_blocks):
        geo_own[pl.ds(me_t * own_blocks + b, 1), 0:4, :] = geo[:, b * BLK:(b + 1) * BLK][None]

    ntaps = taps.shape[0]
    half = (ntaps - 1) // 2
    top = LANES - half
    line = jnp.concatenate(
        [taps[...].astype(f32).reshape(1, ntaps), jnp.zeros((1, 2 * LANES - ntaps), f32)], axis=1)
    slanted = pltpu.roll(jnp.broadcast_to(line, (LANES, 2 * LANES)), 0, 1, stride=1, stride_axis=0)
    toeplitz = jnp.transpose(slanted).astype(bf)
    for w in range(WIN // LANES):
        table[top + w * LANES:top + (w + 2) * LANES, w * LANES:(w + 1) * LANES] = toeplitz

    order = sorted(range(1, tm), key=lambda s: abs(s - tm / 2))
    zc = {}

    def partner(s):
        return lax.rem(me_t + s, tm)

    mine = pl.ds(me_t * own_blocks, own_blocks)

    def filtering(u):
        a, c0, cw = spans[u]
        for s in order + [0]:
            dest = partner(s)
            for w in range(0, cw, WIN):
                n = min(WIN, cw - w)
                at = pl.multiple_of(dest * width + c0 + w, LANES)
                window = padded[:, a:a + TALL, pl.ds(at, n + 2 * LANES)].reshape(own_blocks * TALL, n + 2 * LANES)
                value = jnp.dot(window, table[:n + 2 * LANES, :n], preferred_element_type=f32)
                value = value.astype(bf).reshape(own_blocks, TALL, n)
                if s:
                    filts[u][s - 1, :, :, w:w + n] = value
                else:
                    zs[u][mine, :, w:w + n] = value
        zc[u] = [
            pltpu.make_async_remote_copy(
                filts[u].at[s - 1], zs[u].at[mine],
                z_send.at[u * tm + s], z_recv.at[u * tm + s],
                device_id={"tm": partner(s)}, device_id_type=MESH)
            for s in order
        ]

    for u in range(1):
        loads[spans[u][0]].wait()
        filtering(u)
    pl.semaphore_wait(barrier, tm + nodes - 2)
    my_geo = geo_own.at[mine, pl.ds(0, 4)]
    gz = [
        pltpu.make_async_remote_copy(
            my_geo, my_geo, gz_send.at[s], gz_recv.at[s],
            device_id={"tm": partner(s)}, device_id_type=MESH)
        for s in order
    ]
    for copy in gz:
        copy.start()
    for copy in zc[0]:
        copy.start()
    waited = {spans[0][0]}
    for u in range(1, count):
        if spans[u][0] not in waited:
            loads[spans[u][0]].wait()
            waited.add(spans[u][0])
        filtering(u)
        if u in starts[0]:
            for copy in zc[u]:
                copy.start()
        else:
            @pl.when(inner)
            def _():
                for copy in zc[u]:
                    copy.start()

    for copy in small[2:]:
        copy.wait()

    def chosen(q, k):
        return boundary[0, sends[me_n, q, k]]

    for copy in gz:
        copy.wait_recv()
    gn = []
    for s in range(1, nodes):
        q = lax.rem(me_n + s, nodes)
        for k in range(SEND):
            geo_stage[s * SEND + k] = geo_own[chosen(q, k)]
        copy = pltpu.make_async_remote_copy(
            geo_stage.at[pl.ds(s * SEND, SEND)],
            geo_far.at[pl.ds((nodes - 1 - s) * SEND, SEND)],
            gn_send.at[s], gn_recv.at[s],
            device_id={"node": q}, device_id_type=MESH)
        copy.start()
        gn.append(copy)

    tile = own_blocks * BLK

    def halves(value):
        high = value.astype(bf).astype(f32)
        rest = value - high
        middle = rest.astype(bf).astype(f32)
        return high, middle, rest - middle

    def scaled(block):
        row = lax.broadcasted_iota(jnp.int32, block.shape, 0)
        point = jnp.where(row < 3, (block - 0.5) * (1.0 / SUPPORT_RADIUS), 0.0)
        norm = jnp.broadcast_to(jnp.sum(point * point, axis=0, keepdims=True), block.shape)
        return row, point, norm

    def left(block):
        row, point, norm = scaled(block)
        high, middle, low = halves(jnp.where(row < 3, -2.0 * point, jnp.where(row == 3, norm, jnp.where(row == 4, 1.0, 0.0))))
        return jnp.concatenate([high, high, middle, middle, high, low], axis=0)

    def right(block):
        row, point, norm = scaled(block)
        high, middle, low = halves(jnp.where(row < 3, point, jnp.where(row == 3, 1.0, jnp.where(row == 4, norm, 0.0))))
        return jnp.concatenate([high, middle, high, middle, low, high], axis=0)

    def row_step(r, carry):
        block = geo_own[r]
        at = pl.ds(pl.multiple_of(r * BLK, BLK), BLK)
        rowmat[at, :] = jnp.transpose(left(block)).astype(bf)
        amps[at, :] = jnp.transpose(jnp.broadcast_to(block[3:4] * (1.0 / math.sqrt(nnz)), (BLK, BLK)))
        return carry

    def prepare(is_far):
        source, blocks = (geo_far, slots) if is_far else (geo_own, part_blocks)
        joined = jnp.concatenate([source[g, :, a:a + TALL] for a in groups for g in range(blocks)], axis=1)
        (far_cols if is_far else near_cols)[...] = right(joined).astype(bf)
        lane = lax.broadcasted_iota(jnp.int32, (part_blocks, blocks * TALL), 1)
        name = lax.shift_right_logical(lane, TALL.bit_length() - 1)
        if is_far:
            owner = me_n + 1 + lax.shift_right_logical(name, 2)
            owner = jnp.where(owner >= nodes, owner - nodes, owner)
            name = part_blocks + owner * SEND + jnp.bitwise_and(name, SEND - 1)
        total = jnp.zeros(name.shape, f32)
        for k in range(nloc, nnz) if is_far else range(nloc):
            total = total + jnp.where(cols[:, k:k + 1] == name, 1.0, 0.0)
        total = jnp.concatenate([total] * len(groups), axis=1)
        (far_weight if is_far else near_weight)[...] = total * joined[3:4]

    def build(is_far):
        column = far_cols if is_far else near_cols
        weights = far_weight if is_far else near_weight
        target = far_kern if is_far else near_kern

        def step(t, carry):
            at = pl.ds(pl.multiple_of(t * tile, tile), tile)
            for lo in range(0, column.shape[1], 3 * LANES):
                part = slice(lo, min(lo + 3 * LANES, column.shape[1]))
                square = jnp.dot(rowmat[at, :], column[:, part], preferred_element_type=f32)
                for b in range(own_blocks):
                    value = jnp.maximum(square[b * BLK:(b + 1) * BLK], 1e-30)
                    falloff = jnp.maximum(1.0 - value * lax.rsqrt(value), 0.0)
                    power = falloff * falloff
                    weight = weights[pl.ds(t * own_blocks + b, 1), part]
                    target[pl.ds(pl.multiple_of(t * tile + b * BLK, BLK), BLK), part] = (
                        power * power * (5.0 * weight - (4.0 * weight) * falloff)).astype(bf)
            return carry
        lax.fori_loop(0, part_blocks // own_blocks, step, 0)

    nc, sent = {}, []

    def forward(u):
        for copy in zc[u]:
            copy.wait_recv()
        if starts[u + 1]:
            @pl.when(jnp.logical_not(inner))
            def _():
                for v in starts[u + 1]:
                    for copy in zc[v]:
                        copy.start()
        nc[u] = []
        for s in range(1, nodes):
            q = lax.rem(me_n + s, nodes)
            for k in range(SEND):
                stages[u][s * SEND + k] = zs[u][chosen(q, k)]
            copy = pltpu.make_async_remote_copy(
                stages[u].at[pl.ds(s * SEND, SEND)],
                fars[u].at[pl.ds((nodes - 1 - s) * SEND, SEND)],
                n_send.at[u * nodes + s], n_recv.at[u * nodes + s],
                device_id={"node": q}, device_id_type=MESH)
            copy.start()
            nc[u].append(copy)
            sent.append(copy)

    def add(is_far, picked, c0, cw, first=False, last=False):
        held = [[u for u, (a, p0, pw) in enumerate(spans)
                 if a == group * TALL and p0 < c0 + cw and c0 < p0 + pw] for group in picked]
        if is_far:
            for u in sum(held, []):
                if u in nc:
                    for copy in nc.pop(u):
                        copy.wait_recv()
        refs = fars if is_far else zs
        blocks = slots if is_far else part_blocks
        deep = blocks * TALL
        kern = far_kern if is_far else near_kern

        def step(r, carry):
            at = pl.ds(pl.multiple_of(r * 2 * tile, 2 * tile), 2 * tile)
            right = jnp.concatenate([
                jnp.concatenate([
                    refs[u][:, :, max(c0 - spans[u][1], 0):min(c0 + cw - spans[u][1], spans[u][2])]
                    for u in row
                ], axis=2).reshape(deep, cw)
                for row in held
            ], axis=0)
            total = jnp.dot(
                kern[at, picked[0] * deep:(picked[-1] + 1) * deep], right, preferred_element_type=f32)
            if not first:
                total = total + partial[at, c0:c0 + cw]
            if last:
                scale = jnp.concatenate([amps[at, :]] * (cw // LANES), axis=1)
                out[at, c0:c0 + cw] = (total * scale).astype(bf)
            else:
                partial[at, c0:c0 + cw] = total
            return carry
        lax.fori_loop(0, part_blocks // own_blocks // 2, step, 0)

    def near():
        lax.fori_loop(0, part_blocks, row_step, 0, unroll=4)
        prepare(False)
        build(False)

    def far():
        for copy in gn:
            copy.wait_recv()
        prepare(True)
        build(True)

    forward(0)
    near()
    forward(1)
    far()
    forward(2)
    forward(3)
    add(False, [0, 1], 0, width, first=True)
    forward(4)
    add(True, [0, 1], 0, width)
    forward(5)
    add(False, [2], 0, width)
    forward(6)
    add(True, [2], 0, width)
    forward(7)
    forward(8)
    add(False, [3], 0, width)
    add(True, [3], *spans[6][1:], last=True)
    add(True, [3], *spans[7][1:], last=True)
    add(True, [3], *spans[8][1:], last=True)

    for copy in gz + gn:
        copy.wait_send()
    for u in range(count):
        for copy in zc[u]:
            copy.wait_send()
    for copy in sent:
        copy.wait_send()


def on_device(field, node_geometry, taps, boundary, sends, cols):
    tm = lax.axis_size("tm")
    nodes = lax.axis_size("node")
    rows, steps = field.shape
    part_blocks, nnz = cols.shape
    nloc = nnz - 4
    if part_blocks > nloc:
        return wide_on_device(field, node_geometry, taps, boundary, sends, cols)
    own_blocks = rows // BLK
    width = steps // tm
    sizes = (tm, nodes, width, part_blocks, nnz, nloc, own_blocks)
    spans = plan(width)
    groups = range(0, BLK, TALL)
    count = len(spans)
    slab = part_blocks * BLK
    slots = (nodes - 1) * SEND
    bf, f32 = jnp.bfloat16, jnp.float32
    dma = pltpu.SemaphoreType.DMA
    return pl.pallas_call(
        functools.partial(body, sizes),
        out_shape=pltpu.VMEM((slab, width), bf),
        in_specs=[pl.BlockSpec(memory_space=pl.ANY)] * 6,
        out_specs=pl.BlockSpec(memory_space=pltpu.VMEM),
        scratch_shapes=[
            pltpu.VMEM(node_geometry.shape, f32),
            pltpu.VMEM(taps.shape, bf),
            pltpu.SMEM(boundary.shape, jnp.int32),
            pltpu.SMEM(sends.shape, jnp.int32),
            pltpu.VMEM(cols.shape, jnp.int32),
            pltpu.VMEM((own_blocks, BLK, steps + 2 * LANES), bf),
            pltpu.VMEM((WIN + 2 * LANES, WIN), bf),
            pltpu.VMEM((slab, width), f32),
            pltpu.VMEM((slab, LANES), f32),
            pltpu.VMEM((part_blocks, 8, BLK), f32),
            pltpu.VMEM((nodes * SEND, 8, BLK), f32),
            pltpu.VMEM((slots, 8, BLK), f32),
            pltpu.VMEM((slab, 48), bf),
            *[pltpu.VMEM((tm - 1, own_blocks, TALL, cw), bf) for _, _, cw in spans],
            *[pltpu.VMEM((part_blocks, TALL, cw), bf) for _, _, cw in spans],
            *[pltpu.VMEM((nodes * SEND, TALL, cw), bf) for _, _, cw in spans],
            *[pltpu.VMEM((slots, TALL, cw), bf) for _, _, cw in spans],
            pltpu.VMEM((slab, slab), bf), pltpu.VMEM((slab, slots * BLK), bf),
            pltpu.VMEM((48, slab), bf), pltpu.VMEM((48, slots * BLK), bf),
            pltpu.VMEM((part_blocks, slab), f32), pltpu.VMEM((part_blocks, slots * BLK), f32),
            dma((5,)), dma((len(groups),)),
            dma((tm,)), dma((tm,)),
            dma((nodes,)), dma((nodes,)),
            dma((count * tm,)), dma((count * tm,)),
            dma((count * nodes,)), dma((count * nodes,)),
        ],
        compiler_params=pltpu.CompilerParams(
            collective_id=0, has_side_effects=True, vmem_limit_bytes=58 * 1024 * 1024
        ),
    )(field.reshape(own_blocks, BLK, steps), node_geometry, taps, boundary, sends, cols)


def solution(mesh):
    return jax.shard_map(
        on_device,
        mesh=mesh,
        in_specs=(
            P(("parts", "node", "tm"), None),
            P(None, ("node", "tm")),
            P(),
            P("node", None),
            P(),
            P("node", None),
        ),
        out_specs=P(("parts", "node"), "tm"),
        check_vma=False,
    )
```

```python
import functools
import math

import jax
import jax.numpy as jnp
from jax import lax
from jax.experimental import pallas as pl
from jax.experimental.pallas import tpu as pltpu
from jax.sharding import PartitionSpec as P

BLK = 128
SEND = 4
LANES = 128
MESH = pl.DeviceIdType.MESH
SUPPORT_RADIUS = 0.2


def wide_pieces(chunks):
    counts = ([1] * chunks + [1, 1, 2, 4])[-chunks:] if chunks <= 4 else [1] * (chunks - 2) + [2, 4]
    return [(c, h, counts[c]) for c in range(chunks) for h in range(counts[c])]


def wide_body(
    sizes, field, geo, taps, boundary, sends, cols, out,
    padded, table, partial, filt, geo_own, geo_stage, geo_far, kern, *rest,
):
    tm, nodes, chunks, part_blocks, nnz, nloc, own_blocks = sizes
    rest = list(rest)
    parts = wide_pieces(chunks)
    zs = [rest.pop(0) for _ in parts]
    stages = [rest.pop(0) for _ in parts]
    fars = [rest.pop(0) for _ in parts]
    outs = [rest.pop(0) for _ in range(chunks)]
    (load_sem, own_sem, out_sem, gz_send, gz_recv, gn_send, gn_recv,
     z_send, z_recv, n_send, n_recv) = rest
    me_t = lax.axis_index("tm")
    me_n = lax.axis_index("node")
    rows = own_blocks * BLK
    steps = tm * chunks * LANES

    load = pltpu.make_async_copy(field, padded.at[:, pl.ds(LANES, steps)], load_sem)
    load.start()

    barrier = pltpu.get_barrier_semaphore()
    for s in range(1, tm):
        pl.semaphore_signal(barrier, inc=1, device_id={"tm": lax.rem(me_t + s, tm)}, device_id_type=MESH)
    for s in range(1, nodes):
        pl.semaphore_signal(barrier, inc=1, device_id={"node": lax.rem(me_n + s, nodes)}, device_id_type=MESH)

    padded[:, :LANES] = jnp.zeros((rows, LANES), padded.dtype)
    padded[:, LANES + steps:] = jnp.zeros((rows, LANES), padded.dtype)
    for b in range(own_blocks):
        geo_own[pl.ds(me_t * own_blocks + b, 1), 0:4, :] = geo[:, b * BLK:(b + 1) * BLK][None]
    ntaps = taps.shape[0]
    half = (ntaps - 1) // 2
    top = LANES - half
    span = LANES + 2 * half
    lag = (
        lax.broadcasted_iota(jnp.int32, (span, LANES), 0)
        - lax.broadcasted_iota(jnp.int32, (span, LANES), 1)
    )
    table[:top, :] = jnp.zeros((top, LANES), table.dtype)
    table[top + span:, :] = jnp.zeros((top, LANES), table.dtype)
    table[top:top + span, :] = lax.fori_loop(
        0, ntaps, lambda d, acc: jnp.where(lag == d, taps[d], acc),
        jnp.zeros((span, LANES), jnp.float32),
    ).astype(table.dtype)
    pl.semaphore_wait(barrier, tm + nodes - 2)

    my_geo = geo_own.at[pl.ds(me_t * own_blocks, own_blocks)]
    gz = [
        pltpu.make_async_remote_copy(
            my_geo, my_geo, gz_send.at[s], gz_recv.at[s],
            device_id={"tm": lax.rem(me_t + s, tm)}, device_id_type=MESH)
        for s in range(1, tm)
    ]
    for copy in gz:
        copy.start()
    load.wait()

    order = sorted(range(1, tm), key=lambda s: abs(s - tm / 2))
    zc = []
    for c in range(chunks):
        for s in order + [0]:
            dest = lax.rem(me_t + s, tm)
            at = pl.multiple_of((dest * chunks + c) * LANES, LANES)
            value = jnp.dot(
                padded[:, pl.ds(at, 3 * LANES)], table[...], preferred_element_type=jnp.float32
            ).astype(jnp.bfloat16).reshape(own_blocks, BLK, LANES)
            filt[c * tm + s] = value
        for u, (_, h, count) in enumerate(parts):
            if parts[u][0] != c:
                continue
            height = BLK // count
            mine = pl.ds(me_t * own_blocks, own_blocks)
            for s in order:
                copy = pltpu.make_async_remote_copy(
                    filt.at[c * tm + s, :, pl.ds(h * height, height)],
                    zs[u].at[mine],
                    z_send.at[u * tm + s], z_recv.at[u * tm + s],
                    device_id={"tm": lax.rem(me_t + s, tm)}, device_id_type=MESH)
                if u < 2:
                    copy.start()
                zc.append((u, copy))
            zs[u][mine] = filt[c * tm, :, h * height:(h + 1) * height, :]

    def chosen(q, k):
        return boundary[0, sends[me_n, q, k]]

    for copy in gz:
        copy.wait_recv()
    gn = []
    for s in range(1, nodes):
        q = lax.rem(me_n + s, nodes)
        for k in range(SEND):
            geo_stage[s * SEND + k] = geo_own[chosen(q, k)]
        copy = pltpu.make_async_remote_copy(
            geo_stage.at[pl.ds(s * SEND, SEND)],
            geo_far.at[pl.ds((nodes - 1 - s) * SEND, SEND)],
            gn_send.at[s], gn_recv.at[s],
            device_id={"node": q}, device_id_type=MESH)
        copy.start()
        gn.append(copy)

    slots = (nodes - 1) * SEND
    dense = part_blocks <= nloc

    def far_slot(value):
        at = jnp.maximum(value - part_blocks, 0)
        src = lax.rem(at // SEND + nodes - 1 - me_n, nodes)
        return jnp.minimum(src * SEND + lax.rem(at, SEND), slots - 1)

    def build(lo, hi):
        def step(r, carry):
            mine = geo_own[r]
            spread = [
                jnp.transpose(jnp.broadcast_to(mine[axis:axis + 1], (BLK, BLK)))
                for axis in range(4)
            ]
            row = [v * (1.0 / SUPPORT_RADIUS) for v in spread[:3]]
            amp = spread[3] * (1.0 / math.sqrt(nnz))
            for g in range(lo, hi):
                if dense:
                    if g < part_blocks:
                        other, name, among = geo_own[g], g, range(nloc)
                    else:
                        rel, slot = divmod(g - part_blocks, SEND)
                        other, among = geo_far[g - part_blocks], range(nloc, nnz)
                        name = part_blocks + lax.rem(me_n + 1 + rel, nodes) * SEND + slot
                    count = 0
                    for k in among:
                        count = count + (cols[r, k] == name).astype(jnp.int32)
                    weight = other[3:4] * count.astype(jnp.float32)
                else:
                    if g < nloc:
                        other = geo_own[cols[r, g]]
                    else:
                        other = geo_far[far_slot(cols[r, g])]
                    weight = other[3:4]
                total = None
                for axis in range(3):
                    diff = row[axis] - other[axis:axis + 1] * (1.0 / SUPPORT_RADIUS)
                    total = diff * diff if total is None else total + diff * diff
                scaled = total * lax.rsqrt(jnp.maximum(total, 1e-30))
                falloff = jnp.maximum(1.0 - scaled, 0.0)
                square = falloff * falloff
                values = square * square * (4.0 * scaled + 1.0)
                kern[r, :, g * BLK:(g + 1) * BLK] = (amp * weight * values).astype(jnp.bfloat16)
            return carry
        lax.fori_loop(0, part_blocks, step, 0)

    nc = []

    ahead = {u: (u + 2,) for u in range(len(parts))}
    if len(parts) == 8:
        ahead = {0: (2, 3), 1: (4, 5), 2: (6,), 3: (7,)}

    def forward(u):
        for at, copy in zc:
            if at == u:
                copy.wait_recv()
        for at, copy in zc:
            if at in ahead.get(u, ()):
                copy.start()
        for s in range(1, nodes):
            q = lax.rem(me_n + s, nodes)
            for k in range(SEND):
                stages[u][s * SEND + k] = zs[u][chosen(q, k)]
            copy = pltpu.make_async_remote_copy(
                stages[u].at[pl.ds(s * SEND, SEND)],
                fars[u].at[pl.ds((nodes - 1 - s) * SEND, SEND)],
                n_send.at[u * nodes + s], n_recv.at[u * nodes + s],
                device_id={"node": q}, device_id_type=MESH)
            copy.start()
            nc.append((u, copy))

    outc = []

    split = part_blocks if dense else nloc
    width = part_blocks + slots if dense else nnz
    tile = own_blocks if dense else 1

    def of(c):
        return [u for u, piece in enumerate(parts) if piece[0] == c]

    def product(r, c, lo, hi):
        if dense:
            source = zs if lo == 0 else fars
            right = jnp.concatenate(
                [source[u][...] for u in of(c)], axis=1
            ).reshape((hi - lo) * BLK, LANES)
        else:
            right = jnp.concatenate([
                zs[u][cols[r, k]] if k < nloc else fars[u][far_slot(cols[r, k])]
                for k in range(lo, hi) for u in of(c)
            ], axis=0)
        left = kern[pl.ds(r * tile, tile), :, lo * BLK:hi * BLK]
        return jnp.dot(
            left.reshape(tile * BLK, (hi - lo) * BLK), right,
            preferred_element_type=jnp.float32)

    def local(c):
        def step(r, carry):
            partial[pl.ds(r * tile, tile)] = product(r, c, 0, split).reshape(tile, BLK, LANES)
            return carry
        lax.fori_loop(0, part_blocks // tile, step, 0)

    def far(c):
        for at, copy in nc:
            if parts[at][0] == c:
                copy.wait_recv()

        def step(r, carry):
            total = partial[pl.ds(r * tile, tile)].reshape(tile * BLK, LANES) + product(r, c, split, width)
            outs[c][pl.ds(pl.multiple_of(r * tile * BLK, tile * BLK), tile * BLK), :] = total.astype(jnp.bfloat16)
            return carry
        lax.fori_loop(0, part_blocks // tile, step, 0)
        copy = pltpu.make_async_copy(outs[c], out.at[:, pl.ds(c * LANES, LANES)], out_sem.at[c])
        copy.start()
        outc.append(copy)

    build(0, split)
    for u in of(0)[:1]:
        forward(u)
    for copy in gn:
        copy.wait_recv()
    build(split, width)
    for u in of(0)[1:]:
        forward(u)
    local(0)
    for c in range(1, chunks):
        todo = of(c)
        for u in todo[:-1] if len(todo) > 2 else todo[:1]:
            forward(u)
        far(c - 1)
        for u in todo[-1:] if len(todo) > 1 else []:
            forward(u)
        local(c)
    far(chunks - 1)

    for copy in gz + gn:
        copy.wait_send()
    for _, copy in zc + nc:
        copy.wait_send()
    for copy in outc:
        copy.wait()


def wide_on_device(field, node_geometry, taps, boundary, sends, cols):
    tm = lax.axis_size("tm")
    nodes = lax.axis_size("node")
    rows, steps = field.shape
    part_blocks, nnz = cols.shape
    nloc = nnz - 4
    own_blocks = rows // BLK
    chunks = steps // tm // LANES
    parts = wide_pieces(chunks)
    sizes = (tm, nodes, chunks, part_blocks, nnz, nloc, own_blocks)
    slab = part_blocks * BLK
    slots = (nodes - 1) * SEND
    width = part_blocks + slots if part_blocks <= nloc else nnz
    bf = jnp.bfloat16
    dma = pltpu.SemaphoreType.DMA
    return pl.pallas_call(
        functools.partial(wide_body, sizes),
        out_shape=pltpu.VMEM((slab, steps // tm), bf),
        in_specs=[
            pl.BlockSpec(memory_space=pl.ANY),
            pl.BlockSpec(memory_space=pltpu.VMEM),
            pl.BlockSpec(memory_space=pltpu.SMEM),
            pl.BlockSpec(memory_space=pltpu.SMEM),
            pl.BlockSpec(memory_space=pltpu.SMEM),
            pl.BlockSpec(memory_space=pltpu.SMEM),
        ],
        out_specs=pl.BlockSpec(memory_space=pltpu.VMEM),
        scratch_shapes=[
            pltpu.VMEM((rows, steps + 2 * LANES), bf),
            pltpu.VMEM((3 * LANES, LANES), bf),
            pltpu.VMEM((part_blocks, BLK, LANES), jnp.float32),
            pltpu.VMEM((chunks * tm, own_blocks, BLK, LANES), bf),
            pltpu.VMEM((part_blocks, 8, BLK), jnp.float32),
            pltpu.VMEM((nodes * SEND, 8, BLK), jnp.float32),
            pltpu.VMEM((slots, 8, BLK), jnp.float32),
            pltpu.VMEM((part_blocks, BLK, width * BLK), bf),
            *[pltpu.VMEM((part_blocks, BLK // p[2], LANES), bf) for p in parts],
            *[pltpu.VMEM((nodes * SEND, BLK // p[2], LANES), bf) for p in parts],
            *[pltpu.VMEM((slots, BLK // p[2], LANES), bf) for p in parts],
            *[pltpu.VMEM((slab, LANES), bf) for _ in range(chunks)],
            dma, dma,
            dma((chunks,)),
            dma((tm,)), dma((tm,)),
            dma((nodes,)), dma((nodes,)),
            dma((len(parts) * tm,)), dma((len(parts) * tm,)),
            dma((len(parts) * nodes,)), dma((len(parts) * nodes,)),
        ],
        compiler_params=pltpu.CompilerParams(
            collective_id=0, has_side_effects=True, vmem_limit_bytes=58 * 1024 * 1024
        ),
    )(field, node_geometry, taps.astype(jnp.float32), boundary, sends, cols)


WIN = 256


TALL = 32


def plan(width):
    parts = [(0, 0, 2), (0, 2, 2), (1, 0, 2), (1, 2, 2), (2, 0, 2), (2, 2, 2), (3, 0, 2), (3, 2, 1), (3, 3, 1)]
    unit = width // 4
    spans = [(group * TALL, at * unit, wide * unit) for group, at, wide in parts]
    return spans


WINDOW = 4


def ahead(spans):
    unit = spans[-1][2]
    order, flying, at = [], 0, 0
    for u in range(-1, len(spans)):
        if u >= 0:
            flying -= spans[u][2]
        starts = []
        while at < len(spans) and (flying == 0 or flying + spans[at][2] <= WINDOW * unit):
            starts.append(at)
            flying += spans[at][2]
            at += 1
        order.append(starts)
    return order


def body(
    sizes, field, geo_in, taps_in, boundary_in, sends_in, cols_in, out,
    geo, taps, boundary, sends, cols, padded, table, partial, amps, geo_own, geo_stage, geo_far, rowmat, *rest,
):
    tm, nodes, width, part_blocks, nnz, nloc, own_blocks = sizes
    spans = plan(width)
    groups = range(0, BLK, TALL)
    count = len(spans)
    starts = ahead(spans)
    rest = list(rest)
    filts = [rest.pop(0) for _ in spans]
    zs = [rest.pop(0) for _ in spans]
    stages = [rest.pop(0) for _ in spans]
    fars = [rest.pop(0) for _ in spans]
    (near_kern, far_kern, near_cols, far_cols, near_weight, far_weight, small_sem, load_sem, gz_send, gz_recv, gn_send, gn_recv, z_send, z_recv, n_send, n_recv) = rest
    me_t = lax.axis_index("tm")
    me_n = lax.axis_index("node")
    inner = jnp.logical_and(me_t > 0, me_t < tm - 1)
    steps = tm * width
    slots = (nodes - 1) * SEND
    f32, bf = jnp.float32, jnp.bfloat16

    barrier = pltpu.get_barrier_semaphore()
    for s in range(1, tm):
        pl.semaphore_signal(barrier, inc=1, device_id={"tm": lax.rem(me_t + s, tm)}, device_id_type=MESH)
    for s in range(1, nodes):
        pl.semaphore_signal(barrier, inc=1, device_id={"node": lax.rem(me_n + s, nodes)}, device_id_type=MESH)

    small = [
        pltpu.make_async_copy(source, target, small_sem.at[i])
        for i, (source, target) in enumerate((
            (taps_in, taps), (geo_in, geo), (boundary_in, boundary), (sends_in, sends), (cols_in, cols)))
    ]
    for copy in small[:1]:
        copy.start()
    loads = {}
    for i, a in enumerate(groups):
        loads[a] = pltpu.make_async_copy(
            field.at[:, pl.ds(a, TALL)], padded.at[:, pl.ds(a, TALL), pl.ds(LANES, steps)], load_sem.at[i])
        loads[a].start()
    for copy in small[1:]:
        copy.start()

    padded[:, :, :LANES] = jnp.zeros((own_blocks, BLK, LANES), bf)
    padded[:, :, LANES + steps:] = jnp.zeros((own_blocks, BLK, LANES), bf)
    table[...] = jnp.zeros(table.shape, bf)
    small[0].wait()
    small[1].wait()
    for b in range(own_blocks):
        geo_own[pl.ds(me_t * own_blocks + b, 1), 0:4, :] = geo[:, b * BLK:(b + 1) * BLK][None]

    ntaps = taps.shape[0]
    half = (ntaps - 1) // 2
    top = LANES - half
    line = jnp.concatenate(
        [taps[...].astype(f32).reshape(1, ntaps), jnp.zeros((1, 2 * LANES - ntaps), f32)], axis=1)
    slanted = pltpu.roll(jnp.broadcast_to(line, (LANES, 2 * LANES)), 0, 1, stride=1, stride_axis=0)
    toeplitz = jnp.transpose(slanted).astype(bf)
    for w in range(WIN // LANES):
        table[top + w * LANES:top + (w + 2) * LANES, w * LANES:(w + 1) * LANES] = toeplitz

    order = sorted(range(1, tm), key=lambda s: abs(s - tm / 2))
    zc = {}

    def partner(s):
        return lax.rem(me_t + s, tm)

    mine = pl.ds(me_t * own_blocks, own_blocks)

    def filtering(u):
        a, c0, cw = spans[u]
        for s in order + [0]:
            dest = partner(s)
            for w in range(0, cw, WIN):
                n = min(WIN, cw - w)
                at = pl.multiple_of(dest * width + c0 + w, LANES)
                window = padded[:, a:a + TALL, pl.ds(at, n + 2 * LANES)].reshape(own_blocks * TALL, n + 2 * LANES)
                value = jnp.dot(window, table[:n + 2 * LANES, :n], preferred_element_type=f32)
                value = value.astype(bf).reshape(own_blocks, TALL, n)
                if s:
                    filts[u][s - 1, :, :, w:w + n] = value
                else:
                    zs[u][mine, :, w:w + n] = value
        zc[u] = [
            pltpu.make_async_remote_copy(
                filts[u].at[s - 1], zs[u].at[mine],
                z_send.at[u * tm + s], z_recv.at[u * tm + s],
                device_id={"tm": partner(s)}, device_id_type=MESH)
            for s in order
        ]

    for u in range(1):
        loads[spans[u][0]].wait()
        filtering(u)
    pl.semaphore_wait(barrier, tm + nodes - 2)
    my_geo = geo_own.at[mine, pl.ds(0, 4)]
    gz = [
        pltpu.make_async_remote_copy(
            my_geo, my_geo, gz_send.at[s], gz_recv.at[s],
            device_id={"tm": partner(s)}, device_id_type=MESH)
        for s in order
    ]
    for copy in gz:
        copy.start()
    for copy in zc[0]:
        copy.start()
    waited = {spans[0][0]}
    for u in range(1, count):
        if spans[u][0] not in waited:
            loads[spans[u][0]].wait()
            waited.add(spans[u][0])
        filtering(u)
        if u in starts[0]:
            for copy in zc[u]:
                copy.start()
        else:
            @pl.when(inner)
            def _():
                for copy in zc[u]:
                    copy.start()

    for copy in small[2:]:
        copy.wait()

    def chosen(q, k):
        return boundary[0, sends[me_n, q, k]]

    for copy in gz:
        copy.wait_recv()
    gn = []
    for s in range(1, nodes):
        q = lax.rem(me_n + s, nodes)
        for k in range(SEND):
            geo_stage[s * SEND + k] = geo_own[chosen(q, k)]
        copy = pltpu.make_async_remote_copy(
            geo_stage.at[pl.ds(s * SEND, SEND)],
            geo_far.at[pl.ds((nodes - 1 - s) * SEND, SEND)],
            gn_send.at[s], gn_recv.at[s],
            device_id={"node": q}, device_id_type=MESH)
        copy.start()
        gn.append(copy)

    tile = own_blocks * BLK

    def halves(value):
        high = value.astype(bf).astype(f32)
        rest = value - high
        middle = rest.astype(bf).astype(f32)
        return high, middle, rest - middle

    def scaled(block):
        row = lax.broadcasted_iota(jnp.int32, block.shape, 0)
        point = jnp.where(row < 3, (block - 0.5) * (1.0 / SUPPORT_RADIUS), 0.0)
        norm = jnp.broadcast_to(jnp.sum(point * point, axis=0, keepdims=True), block.shape)
        return row, point, norm

    def left(block):
        row, point, norm = scaled(block)
        high, middle, low = halves(jnp.where(row < 3, -2.0 * point, jnp.where(row == 3, norm, jnp.where(row == 4, 1.0, 0.0))))
        return jnp.concatenate([high, high, middle, middle, high, low], axis=0)

    def right(block):
        row, point, norm = scaled(block)
        high, middle, low = halves(jnp.where(row < 3, point, jnp.where(row == 3, 1.0, jnp.where(row == 4, norm, 0.0))))
        return jnp.concatenate([high, middle, high, middle, low, high], axis=0)

    def row_step(r, carry):
        block = geo_own[r]
        at = pl.ds(pl.multiple_of(r * BLK, BLK), BLK)
        rowmat[at, :] = jnp.transpose(left(block)).astype(bf)
        amps[at, :] = jnp.transpose(jnp.broadcast_to(block[3:4] * (1.0 / math.sqrt(nnz)), (BLK, BLK)))
        return carry

    def prepare(is_far):
        source, blocks = (geo_far, slots) if is_far else (geo_own, part_blocks)
        joined = jnp.concatenate([source[g, :, a:a + TALL] for a in groups for g in range(blocks)], axis=1)
        (far_cols if is_far else near_cols)[...] = right(joined).astype(bf)
        lane = lax.broadcasted_iota(jnp.int32, (part_blocks, blocks * TALL), 1)
        name = lax.shift_right_logical(lane, TALL.bit_length() - 1)
        if is_far:
            owner = me_n + 1 + lax.shift_right_logical(name, 2)
            owner = jnp.where(owner >= nodes, owner - nodes, owner)
            name = part_blocks + owner * SEND + jnp.bitwise_and(name, SEND - 1)
        total = jnp.zeros(name.shape, f32)
        for k in range(nloc, nnz) if is_far else range(nloc):
            total = total + jnp.where(cols[:, k:k + 1] == name, 1.0, 0.0)
        total = jnp.concatenate([total] * len(groups), axis=1)
        (far_weight if is_far else near_weight)[...] = total * joined[3:4]

    def build(is_far):
        column = far_cols if is_far else near_cols
        weights = far_weight if is_far else near_weight
        target = far_kern if is_far else near_kern

        def step(t, carry):
            at = pl.ds(pl.multiple_of(t * tile, tile), tile)
            for lo in range(0, column.shape[1], 3 * LANES):
                part = slice(lo, min(lo + 3 * LANES, column.shape[1]))
                square = jnp.dot(rowmat[at, :], column[:, part], preferred_element_type=f32)
                for b in range(own_blocks):
                    value = jnp.maximum(square[b * BLK:(b + 1) * BLK], 1e-30)
                    falloff = jnp.maximum(1.0 - value * lax.rsqrt(value), 0.0)
                    power = falloff * falloff
                    weight = weights[pl.ds(t * own_blocks + b, 1), part]
                    down = pl.ds(pl.multiple_of(t * tile + b * BLK, BLK), BLK)
                    scale = jnp.concatenate([amps[down, :]] * (falloff.shape[1] // LANES), axis=1)
                    target[down, part] = (
                        scale * (power * power * (5.0 * weight - (4.0 * weight) * falloff))).astype(bf)
            return carry
        lax.fori_loop(0, part_blocks // own_blocks, step, 0)

    nc, sent = {}, []

    def forward(u):
        for copy in zc[u]:
            copy.wait_recv()
        if starts[u + 1]:
            @pl.when(jnp.logical_not(inner))
            def _():
                for v in starts[u + 1]:
                    for copy in zc[v]:
                        copy.start()
        nc[u] = []
        for s in range(1, nodes):
            q = lax.rem(me_n + s, nodes)
            for k in range(SEND):
                stages[u][s * SEND + k] = zs[u][chosen(q, k)]
            copy = pltpu.make_async_remote_copy(
                stages[u].at[pl.ds(s * SEND, SEND)],
                fars[u].at[pl.ds((nodes - 1 - s) * SEND, SEND)],
                n_send.at[u * nodes + s], n_recv.at[u * nodes + s],
                device_id={"node": q}, device_id_type=MESH)
            copy.start()
            nc[u].append(copy)
            sent.append(copy)

    def add(is_far, picked, c0, cw, first=False, last=False):
        held = [[u for u, (a, p0, pw) in enumerate(spans)
                 if a == group * TALL and p0 < c0 + cw and c0 < p0 + pw] for group in picked]
        if is_far:
            for u in sum(held, []):
                if u in nc:
                    for copy in nc.pop(u):
                        copy.wait_recv()
        refs = fars if is_far else zs
        blocks = slots if is_far else part_blocks
        deep = blocks * TALL
        kern = far_kern if is_far else near_kern

        def step(r, carry):
            at = pl.ds(pl.multiple_of(r * 2 * tile, 2 * tile), 2 * tile)
            right = jnp.concatenate([
                jnp.concatenate([
                    refs[u][:, :, max(c0 - spans[u][1], 0):min(c0 + cw - spans[u][1], spans[u][2])]
                    for u in row
                ], axis=2).reshape(deep, cw)
                for row in held
            ], axis=0)
            total = jnp.dot(
                kern[at, picked[0] * deep:(picked[-1] + 1) * deep], right, preferred_element_type=f32)
            if not first:
                total = total + partial[at, c0:c0 + cw]
            if last:
                out[at, c0:c0 + cw] = total.astype(bf)
            else:
                partial[at, c0:c0 + cw] = total
            return carry
        lax.fori_loop(0, part_blocks // own_blocks // 2, step, 0)

    def near():
        lax.fori_loop(0, part_blocks, row_step, 0, unroll=4)
        prepare(False)
        build(False)

    def far():
        for copy in gn:
            copy.wait_recv()
        prepare(True)
        build(True)

    forward(0)
    near()
    forward(1)
    far()
    forward(2)
    forward(3)
    add(False, [0, 1], 0, width, first=True)
    forward(4)
    add(True, [0, 1], 0, width)
    forward(5)
    add(False, [2], 0, width)
    forward(6)
    add(True, [2], 0, width)
    forward(7)
    forward(8)
    add(False, [3], 0, width)
    add(True, [3], *spans[6][1:], last=True)
    add(True, [3], *spans[7][1:], last=True)
    add(True, [3], *spans[8][1:], last=True)

    for copy in gz + gn:
        copy.wait_send()
    for u in range(count):
        for copy in zc[u]:
            copy.wait_send()
    for copy in sent:
        copy.wait_send()


def on_device(field, node_geometry, taps, boundary, sends, cols):
    tm = lax.axis_size("tm")
    nodes = lax.axis_size("node")
    rows, steps = field.shape
    part_blocks, nnz = cols.shape
    nloc = nnz - 4
    if part_blocks > nloc:
        return wide_on_device(field, node_geometry, taps, boundary, sends, cols)
    own_blocks = rows // BLK
    width = steps // tm
    sizes = (tm, nodes, width, part_blocks, nnz, nloc, own_blocks)
    spans = plan(width)
    groups = range(0, BLK, TALL)
    count = len(spans)
    slab = part_blocks * BLK
    slots = (nodes - 1) * SEND
    bf, f32 = jnp.bfloat16, jnp.float32
    dma = pltpu.SemaphoreType.DMA
    return pl.pallas_call(
        functools.partial(body, sizes),
        out_shape=pltpu.VMEM((slab, width), bf),
        in_specs=[pl.BlockSpec(memory_space=pl.ANY)] * 6,
        out_specs=pl.BlockSpec(memory_space=pltpu.VMEM),
        scratch_shapes=[
            pltpu.VMEM(node_geometry.shape, f32),
            pltpu.VMEM(taps.shape, bf),
            pltpu.SMEM(boundary.shape, jnp.int32),
            pltpu.SMEM(sends.shape, jnp.int32),
            pltpu.VMEM(cols.shape, jnp.int32),
            pltpu.VMEM((own_blocks, BLK, steps + 2 * LANES), bf),
            pltpu.VMEM((WIN + 2 * LANES, WIN), bf),
            pltpu.VMEM((slab, width), f32),
            pltpu.VMEM((slab, LANES), f32),
            pltpu.VMEM((part_blocks, 8, BLK), f32),
            pltpu.VMEM((nodes * SEND, 8, BLK), f32),
            pltpu.VMEM((slots, 8, BLK), f32),
            pltpu.VMEM((slab, 48), bf),
            *[pltpu.VMEM((tm - 1, own_blocks, TALL, cw), bf) for _, _, cw in spans],
            *[pltpu.VMEM((part_blocks, TALL, cw), bf) for _, _, cw in spans],
            *[pltpu.VMEM((nodes * SEND, TALL, cw), bf) for _, _, cw in spans],
            *[pltpu.VMEM((slots, TALL, cw), bf) for _, _, cw in spans],
            pltpu.VMEM((slab, slab), bf), pltpu.VMEM((slab, slots * BLK), bf),
            pltpu.VMEM((48, slab), bf), pltpu.VMEM((48, slots * BLK), bf),
            pltpu.VMEM((part_blocks, slab), f32), pltpu.VMEM((part_blocks, slots * BLK), f32),
            dma((5,)), dma((len(groups),)),
            dma((tm,)), dma((tm,)),
            dma((nodes,)), dma((nodes,)),
            dma((count * tm,)), dma((count * tm,)),
            dma((count * nodes,)), dma((count * nodes,)),
        ],
        compiler_params=pltpu.CompilerParams(
            collective_id=0, has_side_effects=True, vmem_limit_bytes=58 * 1024 * 1024
        ),
    )(field.reshape(own_blocks, BLK, steps), node_geometry, taps, boundary, sends, cols)


def solution(mesh):
    return jax.shard_map(
        on_device,
        mesh=mesh,
        in_specs=(
            P(("parts", "node", "tm"), None),
            P(None, ("node", "tm")),
            P(),
            P("node", None),
            P(),
            P("node", None),
        ),
        out_specs=P(("parts", "node"), "tm"),
        check_vma=False,
    )
```

```python
import functools
import math

import jax
import jax.numpy as jnp
from jax import lax
from jax.experimental import pallas as pl
from jax.experimental.pallas import tpu as pltpu
from jax.sharding import PartitionSpec as P

BLK = 128
SEND = 4
LANES = 128
MESH = pl.DeviceIdType.MESH
SUPPORT_RADIUS = 0.2


def wide_pieces(chunks):
    counts = ([1] * chunks + [1, 1, 2, 4])[-chunks:] if chunks <= 4 else [1] * (chunks - 2) + [2, 4]
    return [(c, h, counts[c]) for c in range(chunks) for h in range(counts[c])]


def wide_body(
    sizes, field, geo, taps, boundary, sends, cols, out,
    padded, table, partial, filt, geo_own, geo_stage, geo_far, kern, *rest,
):
    tm, nodes, chunks, part_blocks, nnz, nloc, own_blocks = sizes
    rest = list(rest)
    parts = wide_pieces(chunks)
    zs = [rest.pop(0) for _ in parts]
    stages = [rest.pop(0) for _ in parts]
    fars = [rest.pop(0) for _ in parts]
    outs = [rest.pop(0) for _ in range(chunks)]
    (load_sem, own_sem, out_sem, gz_send, gz_recv, gn_send, gn_recv,
     z_send, z_recv, n_send, n_recv) = rest
    me_t = lax.axis_index("tm")
    me_n = lax.axis_index("node")
    rows = own_blocks * BLK
    steps = tm * chunks * LANES

    load = pltpu.make_async_copy(field, padded.at[:, pl.ds(LANES, steps)], load_sem)
    load.start()

    barrier = pltpu.get_barrier_semaphore()
    for s in range(1, tm):
        pl.semaphore_signal(barrier, inc=1, device_id={"tm": lax.rem(me_t + s, tm)}, device_id_type=MESH)
    for s in range(1, nodes):
        pl.semaphore_signal(barrier, inc=1, device_id={"node": lax.rem(me_n + s, nodes)}, device_id_type=MESH)

    padded[:, :LANES] = jnp.zeros((rows, LANES), padded.dtype)
    padded[:, LANES + steps:] = jnp.zeros((rows, LANES), padded.dtype)
    for b in range(own_blocks):
        geo_own[pl.ds(me_t * own_blocks + b, 1), 0:4, :] = geo[:, b * BLK:(b + 1) * BLK][None]
    ntaps = taps.shape[0]
    half = (ntaps - 1) // 2
    top = LANES - half
    span = LANES + 2 * half
    lag = (
        lax.broadcasted_iota(jnp.int32, (span, LANES), 0)
        - lax.broadcasted_iota(jnp.int32, (span, LANES), 1)
    )
    table[:top, :] = jnp.zeros((top, LANES), table.dtype)
    table[top + span:, :] = jnp.zeros((top, LANES), table.dtype)
    table[top:top + span, :] = lax.fori_loop(
        0, ntaps, lambda d, acc: jnp.where(lag == d, taps[d], acc),
        jnp.zeros((span, LANES), jnp.float32),
    ).astype(table.dtype)
    pl.semaphore_wait(barrier, tm + nodes - 2)

    my_geo = geo_own.at[pl.ds(me_t * own_blocks, own_blocks)]
    gz = [
        pltpu.make_async_remote_copy(
            my_geo, my_geo, gz_send.at[s], gz_recv.at[s],
            device_id={"tm": lax.rem(me_t + s, tm)}, device_id_type=MESH)
        for s in range(1, tm)
    ]
    for copy in gz:
        copy.start()
    load.wait()

    order = sorted(range(1, tm), key=lambda s: abs(s - tm / 2))
    zc = []
    for c in range(chunks):
        for s in order + [0]:
            dest = lax.rem(me_t + s, tm)
            at = pl.multiple_of((dest * chunks + c) * LANES, LANES)
            value = jnp.dot(
                padded[:, pl.ds(at, 3 * LANES)], table[...], preferred_element_type=jnp.float32
            ).astype(jnp.bfloat16).reshape(own_blocks, BLK, LANES)
            filt[c * tm + s] = value
        for u, (_, h, count) in enumerate(parts):
            if parts[u][0] != c:
                continue
            height = BLK // count
            mine = pl.ds(me_t * own_blocks, own_blocks)
            for s in order:
                copy = pltpu.make_async_remote_copy(
                    filt.at[c * tm + s, :, pl.ds(h * height, height)],
                    zs[u].at[mine],
                    z_send.at[u * tm + s], z_recv.at[u * tm + s],
                    device_id={"tm": lax.rem(me_t + s, tm)}, device_id_type=MESH)
                if u < 2:
                    copy.start()
                zc.append((u, copy))
            zs[u][mine] = filt[c * tm, :, h * height:(h + 1) * height, :]

    def chosen(q, k):
        return boundary[0, sends[me_n, q, k]]

    for copy in gz:
        copy.wait_recv()
    gn = []
    for s in range(1, nodes):
        q = lax.rem(me_n + s, nodes)
        for k in range(SEND):
            geo_stage[s * SEND + k] = geo_own[chosen(q, k)]
        copy = pltpu.make_async_remote_copy(
            geo_stage.at[pl.ds(s * SEND, SEND)],
            geo_far.at[pl.ds((nodes - 1 - s) * SEND, SEND)],
            gn_send.at[s], gn_recv.at[s],
            device_id={"node": q}, device_id_type=MESH)
        copy.start()
        gn.append(copy)

    slots = (nodes - 1) * SEND
    dense = part_blocks <= nloc

    def far_slot(value):
        at = jnp.maximum(value - part_blocks, 0)
        src = lax.rem(at // SEND + nodes - 1 - me_n, nodes)
        return jnp.minimum(src * SEND + lax.rem(at, SEND), slots - 1)

    def build(lo, hi):
        def step(r, carry):
            mine = geo_own[r]
            spread = [
                jnp.transpose(jnp.broadcast_to(mine[axis:axis + 1], (BLK, BLK)))
                for axis in range(4)
            ]
            row = [v * (1.0 / SUPPORT_RADIUS) for v in spread[:3]]
            amp = spread[3] * (1.0 / math.sqrt(nnz))
            for g in range(lo, hi):
                if dense:
                    if g < part_blocks:
                        other, name, among = geo_own[g], g, range(nloc)
                    else:
                        rel, slot = divmod(g - part_blocks, SEND)
                        other, among = geo_far[g - part_blocks], range(nloc, nnz)
                        name = part_blocks + lax.rem(me_n + 1 + rel, nodes) * SEND + slot
                    count = 0
                    for k in among:
                        count = count + (cols[r, k] == name).astype(jnp.int32)
                    weight = other[3:4] * count.astype(jnp.float32)
                else:
                    if g < nloc:
                        other = geo_own[cols[r, g]]
                    else:
                        other = geo_far[far_slot(cols[r, g])]
                    weight = other[3:4]
                total = None
                for axis in range(3):
                    diff = row[axis] - other[axis:axis + 1] * (1.0 / SUPPORT_RADIUS)
                    total = diff * diff if total is None else total + diff * diff
                scaled = total * lax.rsqrt(jnp.maximum(total, 1e-30))
                falloff = jnp.maximum(1.0 - scaled, 0.0)
                square = falloff * falloff
                values = square * square * (4.0 * scaled + 1.0)
                kern[r, :, g * BLK:(g + 1) * BLK] = (amp * weight * values).astype(jnp.bfloat16)
            return carry
        lax.fori_loop(0, part_blocks, step, 0)

    nc = []

    ahead = {u: (u + 2,) for u in range(len(parts))}
    if len(parts) == 8:
        ahead = {0: (2, 3), 1: (4, 5), 2: (6,), 3: (7,)}

    def forward(u):
        for at, copy in zc:
            if at == u:
                copy.wait_recv()
        for at, copy in zc:
            if at in ahead.get(u, ()):
                copy.start()
        for s in range(1, nodes):
            q = lax.rem(me_n + s, nodes)
            for k in range(SEND):
                stages[u][s * SEND + k] = zs[u][chosen(q, k)]
            copy = pltpu.make_async_remote_copy(
                stages[u].at[pl.ds(s * SEND, SEND)],
                fars[u].at[pl.ds((nodes - 1 - s) * SEND, SEND)],
                n_send.at[u * nodes + s], n_recv.at[u * nodes + s],
                device_id={"node": q}, device_id_type=MESH)
            copy.start()
            nc.append((u, copy))

    outc = []

    split = part_blocks if dense else nloc
    width = part_blocks + slots if dense else nnz
    tile = own_blocks if dense else 1

    def of(c):
        return [u for u, piece in enumerate(parts) if piece[0] == c]

    def product(r, c, lo, hi):
        if dense:
            source = zs if lo == 0 else fars
            right = jnp.concatenate(
                [source[u][...] for u in of(c)], axis=1
            ).reshape((hi - lo) * BLK, LANES)
        else:
            right = jnp.concatenate([
                zs[u][cols[r, k]] if k < nloc else fars[u][far_slot(cols[r, k])]
                for k in range(lo, hi) for u in of(c)
            ], axis=0)
        left = kern[pl.ds(r * tile, tile), :, lo * BLK:hi * BLK]
        return jnp.dot(
            left.reshape(tile * BLK, (hi - lo) * BLK), right,
            preferred_element_type=jnp.float32)

    def local(c):
        def step(r, carry):
            partial[pl.ds(r * tile, tile)] = product(r, c, 0, split).reshape(tile, BLK, LANES)
            return carry
        lax.fori_loop(0, part_blocks // tile, step, 0)

    def far(c):
        for at, copy in nc:
            if parts[at][0] == c:
                copy.wait_recv()

        def step(r, carry):
            total = partial[pl.ds(r * tile, tile)].reshape(tile * BLK, LANES) + product(r, c, split, width)
            outs[c][pl.ds(pl.multiple_of(r * tile * BLK, tile * BLK), tile * BLK), :] = total.astype(jnp.bfloat16)
            return carry
        lax.fori_loop(0, part_blocks // tile, step, 0)
        copy = pltpu.make_async_copy(outs[c], out.at[:, pl.ds(c * LANES, LANES)], out_sem.at[c])
        copy.start()
        outc.append(copy)

    build(0, split)
    for u in of(0)[:1]:
        forward(u)
    for copy in gn:
        copy.wait_recv()
    build(split, width)
    for u in of(0)[1:]:
        forward(u)
    local(0)
    for c in range(1, chunks):
        todo = of(c)
        for u in todo[:-1] if len(todo) > 2 else todo[:1]:
            forward(u)
        far(c - 1)
        for u in todo[-1:] if len(todo) > 1 else []:
            forward(u)
        local(c)
    far(chunks - 1)

    for copy in gz + gn:
        copy.wait_send()
    for _, copy in zc + nc:
        copy.wait_send()
    for copy in outc:
        copy.wait()


def wide_on_device(field, node_geometry, taps, boundary, sends, cols):
    tm = lax.axis_size("tm")
    nodes = lax.axis_size("node")
    rows, steps = field.shape
    part_blocks, nnz = cols.shape
    nloc = nnz - 4
    own_blocks = rows // BLK
    chunks = steps // tm // LANES
    parts = wide_pieces(chunks)
    sizes = (tm, nodes, chunks, part_blocks, nnz, nloc, own_blocks)
    slab = part_blocks * BLK
    slots = (nodes - 1) * SEND
    width = part_blocks + slots if part_blocks <= nloc else nnz
    bf = jnp.bfloat16
    dma = pltpu.SemaphoreType.DMA
    return pl.pallas_call(
        functools.partial(wide_body, sizes),
        out_shape=pltpu.VMEM((slab, steps // tm), bf),
        in_specs=[
            pl.BlockSpec(memory_space=pl.ANY),
            pl.BlockSpec(memory_space=pltpu.VMEM),
            pl.BlockSpec(memory_space=pltpu.SMEM),
            pl.BlockSpec(memory_space=pltpu.SMEM),
            pl.BlockSpec(memory_space=pltpu.SMEM),
            pl.BlockSpec(memory_space=pltpu.SMEM),
        ],
        out_specs=pl.BlockSpec(memory_space=pltpu.VMEM),
        scratch_shapes=[
            pltpu.VMEM((rows, steps + 2 * LANES), bf),
            pltpu.VMEM((3 * LANES, LANES), bf),
            pltpu.VMEM((part_blocks, BLK, LANES), jnp.float32),
            pltpu.VMEM((chunks * tm, own_blocks, BLK, LANES), bf),
            pltpu.VMEM((part_blocks, 8, BLK), jnp.float32),
            pltpu.VMEM((nodes * SEND, 8, BLK), jnp.float32),
            pltpu.VMEM((slots, 8, BLK), jnp.float32),
            pltpu.VMEM((part_blocks, BLK, width * BLK), bf),
            *[pltpu.VMEM((part_blocks, BLK // p[2], LANES), bf) for p in parts],
            *[pltpu.VMEM((nodes * SEND, BLK // p[2], LANES), bf) for p in parts],
            *[pltpu.VMEM((slots, BLK // p[2], LANES), bf) for p in parts],
            *[pltpu.VMEM((slab, LANES), bf) for _ in range(chunks)],
            dma, dma,
            dma((chunks,)),
            dma((tm,)), dma((tm,)),
            dma((nodes,)), dma((nodes,)),
            dma((len(parts) * tm,)), dma((len(parts) * tm,)),
            dma((len(parts) * nodes,)), dma((len(parts) * nodes,)),
        ],
        compiler_params=pltpu.CompilerParams(
            collective_id=0, has_side_effects=True, vmem_limit_bytes=58 * 1024 * 1024
        ),
    )(field, node_geometry, taps.astype(jnp.float32), boundary, sends, cols)


WIN = 256


TALL = 32


def plan(width):
    parts = [(0, 0, 2), (0, 2, 2), (1, 0, 2), (1, 2, 2), (2, 0, 2), (2, 2, 2), (3, 0, 2), (3, 2, 1), (3, 3, 1)]
    unit = width // 4
    spans = [(group * TALL, at * unit, wide * unit) for group, at, wide in parts]
    return spans


WINDOW = 4


def ahead(spans):
    unit = spans[-1][2]
    order, flying, at = [], 0, 0
    for u in range(-1, len(spans)):
        if u >= 0:
            flying -= spans[u][2]
        starts = []
        while at < len(spans) and (flying == 0 or flying + spans[at][2] <= WINDOW * unit):
            starts.append(at)
            flying += spans[at][2]
            at += 1
        order.append(starts)
    return order


def body(
    sizes, field, geo_in, taps_in, boundary_in, sends_in, cols_in, out,
    geo, taps, boundary, sends, cols, padded, table, partial, amps, geo_own, geo_stage, geo_far, rowmat, *rest,
):
    tm, nodes, width, part_blocks, nnz, nloc, own_blocks = sizes
    spans = plan(width)
    groups = range(0, BLK, TALL)
    count = len(spans)
    starts = ahead(spans)
    rest = list(rest)
    filts = [rest.pop(0) for _ in spans]
    zs = [rest.pop(0) for _ in spans]
    stages = [rest.pop(0) for _ in spans]
    fars = [rest.pop(0) for _ in spans]
    (near_kern, far_kern, near_cols, far_cols, near_weight, far_weight, small_sem, load_sem, gz_send, gz_recv, gn_send, gn_recv, z_send, z_recv, n_send, n_recv) = rest
    me_t = lax.axis_index("tm")
    me_n = lax.axis_index("node")
    inner = jnp.logical_and(me_t > 0, me_t < tm - 1)
    steps = tm * width
    slots = (nodes - 1) * SEND
    f32, bf = jnp.float32, jnp.bfloat16

    barrier = pltpu.get_barrier_semaphore()
    for s in range(1, tm):
        pl.semaphore_signal(barrier, inc=1, device_id={"tm": lax.rem(me_t + s, tm)}, device_id_type=MESH)
    for s in range(1, nodes):
        pl.semaphore_signal(barrier, inc=1, device_id={"node": lax.rem(me_n + s, nodes)}, device_id_type=MESH)

    small = [
        pltpu.make_async_copy(source, target, small_sem.at[i])
        for i, (source, target) in enumerate((
            (taps_in, taps), (geo_in, geo), (boundary_in, boundary), (sends_in, sends), (cols_in, cols)))
    ]
    for copy in small[:1]:
        copy.start()
    loads = {}
    for i, a in enumerate(groups):
        loads[a] = pltpu.make_async_copy(
            field.at[:, pl.ds(a, TALL)], padded.at[:, pl.ds(a, TALL), pl.ds(LANES, steps)], load_sem.at[i])
        loads[a].start()
    for copy in small[1:]:
        copy.start()

    padded[:, :, :LANES] = jnp.zeros((own_blocks, BLK, LANES), bf)
    padded[:, :, LANES + steps:] = jnp.zeros((own_blocks, BLK, LANES), bf)
    table[...] = jnp.zeros(table.shape, bf)
    small[0].wait()
    small[1].wait()
    for b in range(own_blocks):
        geo_own[pl.ds(me_t * own_blocks + b, 1), 0:4, :] = geo[:, b * BLK:(b + 1) * BLK][None]

    ntaps = taps.shape[0]
    half = (ntaps - 1) // 2
    top = LANES - half
    line = jnp.concatenate(
        [taps[...].astype(f32).reshape(1, ntaps), jnp.zeros((1, 2 * LANES - ntaps), f32)], axis=1)
    slanted = pltpu.roll(jnp.broadcast_to(line, (LANES, 2 * LANES)), 0, 1, stride=1, stride_axis=0)
    toeplitz = jnp.transpose(slanted).astype(bf)
    for w in range(WIN // LANES):
        table[top + w * LANES:top + (w + 2) * LANES, w * LANES:(w + 1) * LANES] = toeplitz

    order = sorted(range(1, tm), key=lambda s: (s - tm // 2) % (tm - 1))
    zc = {}

    def partner(s):
        return lax.rem(me_t + s, tm)

    mine = pl.ds(me_t * own_blocks, own_blocks)

    def filtering(u):
        a, c0, cw = spans[u]
        for s in order + [0]:
            dest = partner(s)
            for w in range(0, cw, WIN):
                n = min(WIN, cw - w)
                at = pl.multiple_of(dest * width + c0 + w, LANES)
                window = padded[:, a:a + TALL, pl.ds(at, n + 2 * LANES)].reshape(own_blocks * TALL, n + 2 * LANES)
                value = jnp.dot(window, table[:n + 2 * LANES, :n], preferred_element_type=f32)
                value = value.astype(bf).reshape(own_blocks, TALL, n)
                if s:
                    filts[u][s - 1, :, :, w:w + n] = value
                else:
                    zs[u][mine, :, w:w + n] = value
        zc[u] = [
            pltpu.make_async_remote_copy(
                filts[u].at[s - 1], zs[u].at[mine],
                z_send.at[u * tm + s], z_recv.at[u * tm + s],
                device_id={"tm": partner(s)}, device_id_type=MESH)
            for s in order
        ]

    for u in range(1):
        loads[spans[u][0]].wait()
        filtering(u)
    pl.semaphore_wait(barrier, tm + nodes - 2)
    my_geo = geo_own.at[mine, pl.ds(0, 4)]
    gz = [
        pltpu.make_async_remote_copy(
            my_geo, my_geo, gz_send.at[s], gz_recv.at[s],
            device_id={"tm": partner(s)}, device_id_type=MESH)
        for s in order
    ]
    for copy in gz:
        copy.start()
    for copy in zc[0]:
        copy.start()
    waited = {spans[0][0]}
    for u in range(1, count):
        if spans[u][0] not in waited:
            loads[spans[u][0]].wait()
            waited.add(spans[u][0])
        filtering(u)
        if u in starts[0]:
            for copy in zc[u]:
                copy.start()
        else:
            @pl.when(inner)
            def _():
                for copy in zc[u]:
                    copy.start()

    for copy in small[2:]:
        copy.wait()

    def chosen(q, k):
        return boundary[0, sends[me_n, q, k]]

    for copy in gz:
        copy.wait_recv()
    gn = []
    for s in range(1, nodes):
        q = lax.rem(me_n + s, nodes)
        for k in range(SEND):
            geo_stage[s * SEND + k] = geo_own[chosen(q, k)]
        copy = pltpu.make_async_remote_copy(
            geo_stage.at[pl.ds(s * SEND, SEND)],
            geo_far.at[pl.ds((nodes - 1 - s) * SEND, SEND)],
            gn_send.at[s], gn_recv.at[s],
            device_id={"node": q}, device_id_type=MESH)
        copy.start()
        gn.append(copy)

    tile = own_blocks * BLK

    def halves(value):
        high = value.astype(bf).astype(f32)
        rest = value - high
        middle = rest.astype(bf).astype(f32)
        return high, middle, rest - middle

    def scaled(block):
        row = lax.broadcasted_iota(jnp.int32, block.shape, 0)
        point = jnp.where(row < 3, (block - 0.5) * (1.0 / SUPPORT_RADIUS), 0.0)
        norm = jnp.broadcast_to(jnp.sum(point * point, axis=0, keepdims=True), block.shape)
        return row, point, norm

    def left(block):
        row, point, norm = scaled(block)
        high, middle, low = halves(jnp.where(row < 3, -2.0 * point, jnp.where(row == 3, norm, jnp.where(row == 4, 1.0, 0.0))))
        return jnp.concatenate([high, high, middle, middle, high, low], axis=0)

    def right(block):
        row, point, norm = scaled(block)
        high, middle, low = halves(jnp.where(row < 3, point, jnp.where(row == 3, 1.0, jnp.where(row == 4, norm, 0.0))))
        return jnp.concatenate([high, middle, high, middle, low, high], axis=0)

    def row_step(r, carry):
        block = geo_own[r]
        at = pl.ds(pl.multiple_of(r * BLK, BLK), BLK)
        rowmat[at, :] = jnp.transpose(left(block)).astype(bf)
        amps[at, :] = jnp.transpose(jnp.broadcast_to(block[3:4] * (1.0 / math.sqrt(nnz)), (BLK, BLK)))
        return carry

    def prepare(is_far):
        source, blocks = (geo_far, slots) if is_far else (geo_own, part_blocks)
        joined = jnp.concatenate([source[g, :, a:a + TALL] for a in groups for g in range(blocks)], axis=1)
        (far_cols if is_far else near_cols)[...] = right(joined).astype(bf)
        lane = lax.broadcasted_iota(jnp.int32, (part_blocks, blocks * TALL), 1)
        name = lax.shift_right_logical(lane, TALL.bit_length() - 1)
        if is_far:
            owner = me_n + 1 + lax.shift_right_logical(name, 2)
            owner = jnp.where(owner >= nodes, owner - nodes, owner)
            name = part_blocks + owner * SEND + jnp.bitwise_and(name, SEND - 1)
        total = jnp.zeros(name.shape, f32)
        for k in range(nloc, nnz) if is_far else range(nloc):
            total = total + jnp.where(cols[:, k:k + 1] == name, 1.0, 0.0)
        total = jnp.concatenate([total] * len(groups), axis=1)
        (far_weight if is_far else near_weight)[...] = total * joined[3:4]

    def build(is_far):
        column = far_cols if is_far else near_cols
        weights = far_weight if is_far else near_weight
        target = far_kern if is_far else near_kern

        def step(t, carry):
            at = pl.ds(pl.multiple_of(t * tile, tile), tile)
            for lo in range(0, column.shape[1], 3 * LANES):
                part = slice(lo, min(lo + 3 * LANES, column.shape[1]))
                square = jnp.dot(rowmat[at, :], column[:, part], preferred_element_type=f32)
                for b in range(own_blocks):
                    value = jnp.maximum(square[b * BLK:(b + 1) * BLK], 1e-30)
                    falloff = jnp.maximum(1.0 - value * lax.rsqrt(value), 0.0)
                    power = falloff * falloff
                    weight = weights[pl.ds(t * own_blocks + b, 1), part]
                    down = pl.ds(pl.multiple_of(t * tile + b * BLK, BLK), BLK)
                    scale = jnp.concatenate([amps[down, :]] * (falloff.shape[1] // LANES), axis=1)
                    target[down, part] = (
                        scale * (power * power * (5.0 * weight - (4.0 * weight) * falloff))).astype(bf)
            return carry
        lax.fori_loop(0, part_blocks // own_blocks, step, 0)

    nc, sent = {}, []

    def forward(u):
        for copy in zc[u]:
            copy.wait_recv()
        if starts[u + 1]:
            @pl.when(jnp.logical_not(inner))
            def _():
                for v in starts[u + 1]:
                    for copy in zc[v]:
                        copy.start()
        nc[u] = []
        for s in sorted(range(1, nodes), key=lambda s: abs(s - nodes / 2)):
            q = lax.rem(me_n + s, nodes)
            for k in range(SEND):
                stages[u][s * SEND + k] = zs[u][chosen(q, k)]
            copy = pltpu.make_async_remote_copy(
                stages[u].at[pl.ds(s * SEND, SEND)],
                fars[u].at[pl.ds((nodes - 1 - s) * SEND, SEND)],
                n_send.at[u * nodes + s], n_recv.at[u * nodes + s],
                device_id={"node": q}, device_id_type=MESH)
            copy.start()
            nc[u].append(copy)
            sent.append(copy)

    def add(is_far, picked, c0, cw, first=False, last=False):
        held = [[u for u, (a, p0, pw) in enumerate(spans)
                 if a == group * TALL and p0 < c0 + cw and c0 < p0 + pw] for group in picked]
        if is_far:
            for u in sum(held, []):
                if u in nc:
                    for copy in nc.pop(u):
                        copy.wait_recv()
        refs = fars if is_far else zs
        blocks = slots if is_far else part_blocks
        deep = blocks * TALL
        kern = far_kern if is_far else near_kern

        def step(r, carry):
            at = pl.ds(pl.multiple_of(r * 2 * tile, 2 * tile), 2 * tile)
            right = jnp.concatenate([
                jnp.concatenate([
                    refs[u][:, :, max(c0 - spans[u][1], 0):min(c0 + cw - spans[u][1], spans[u][2])]
                    for u in row
                ], axis=2).reshape(deep, cw)
                for row in held
            ], axis=0)
            total = jnp.dot(
                kern[at, picked[0] * deep:(picked[-1] + 1) * deep], right, preferred_element_type=f32)
            if not first:
                total = total + partial[at, c0:c0 + cw]
            if last:
                out[at, c0:c0 + cw] = total.astype(bf)
            else:
                partial[at, c0:c0 + cw] = total
            return carry
        lax.fori_loop(0, part_blocks // own_blocks // 2, step, 0)

    def near():
        lax.fori_loop(0, part_blocks, row_step, 0, unroll=4)
        prepare(False)
        build(False)

    def far():
        for copy in gn:
            copy.wait_recv()
        prepare(True)
        build(True)

    forward(0)
    near()
    forward(1)
    far()
    forward(2)
    forward(3)
    add(False, [0, 1], 0, width, first=True)
    forward(4)
    add(True, [0, 1], 0, width)
    forward(5)
    add(False, [2], 0, width)
    forward(6)
    add(True, [2], 0, width)
    forward(7)
    forward(8)
    add(False, [3], 0, width)
    add(True, [3], *spans[6][1:], last=True)
    add(True, [3], *spans[7][1:], last=True)
    add(True, [3], *spans[8][1:], last=True)

    for copy in gz + gn:
        copy.wait_send()
    for u in range(count):
        for copy in zc[u]:
            copy.wait_send()
    for copy in sent:
        copy.wait_send()


def on_device(field, node_geometry, taps, boundary, sends, cols):
    tm = lax.axis_size("tm")
    nodes = lax.axis_size("node")
    rows, steps = field.shape
    part_blocks, nnz = cols.shape
    nloc = nnz - 4
    if part_blocks > nloc:
        return wide_on_device(field, node_geometry, taps, boundary, sends, cols)
    own_blocks = rows // BLK
    width = steps // tm
    sizes = (tm, nodes, width, part_blocks, nnz, nloc, own_blocks)
    spans = plan(width)
    groups = range(0, BLK, TALL)
    count = len(spans)
    slab = part_blocks * BLK
    slots = (nodes - 1) * SEND
    bf, f32 = jnp.bfloat16, jnp.float32
    dma = pltpu.SemaphoreType.DMA
    return pl.pallas_call(
        functools.partial(body, sizes),
        out_shape=pltpu.VMEM((slab, width), bf),
        in_specs=[pl.BlockSpec(memory_space=pl.ANY)] * 6,
        out_specs=pl.BlockSpec(memory_space=pltpu.VMEM),
        scratch_shapes=[
            pltpu.VMEM(node_geometry.shape, f32),
            pltpu.VMEM(taps.shape, bf),
            pltpu.SMEM(boundary.shape, jnp.int32),
            pltpu.SMEM(sends.shape, jnp.int32),
            pltpu.VMEM(cols.shape, jnp.int32),
            pltpu.VMEM((own_blocks, BLK, steps + 2 * LANES), bf),
            pltpu.VMEM((WIN + 2 * LANES, WIN), bf),
            pltpu.VMEM((slab, width), f32),
            pltpu.VMEM((slab, LANES), f32),
            pltpu.VMEM((part_blocks, 8, BLK), f32),
            pltpu.VMEM((nodes * SEND, 8, BLK), f32),
            pltpu.VMEM((slots, 8, BLK), f32),
            pltpu.VMEM((slab, 48), bf),
            *[pltpu.VMEM((tm - 1, own_blocks, TALL, cw), bf) for _, _, cw in spans],
            *[pltpu.VMEM((part_blocks, TALL, cw), bf) for _, _, cw in spans],
            *[pltpu.VMEM((nodes * SEND, TALL, cw), bf) for _, _, cw in spans],
            *[pltpu.VMEM((slots, TALL, cw), bf) for _, _, cw in spans],
            pltpu.VMEM((slab, slab), bf), pltpu.VMEM((slab, slots * BLK), bf),
            pltpu.VMEM((48, slab), bf), pltpu.VMEM((48, slots * BLK), bf),
            pltpu.VMEM((part_blocks, slab), f32), pltpu.VMEM((part_blocks, slots * BLK), f32),
            dma((5,)), dma((len(groups),)),
            dma((tm,)), dma((tm,)),
            dma((nodes,)), dma((nodes,)),
            dma((count * tm,)), dma((count * tm,)),
            dma((count * nodes,)), dma((count * nodes,)),
        ],
        compiler_params=pltpu.CompilerParams(
            collective_id=0, has_side_effects=True, vmem_limit_bytes=58 * 1024 * 1024
        ),
    )(field.reshape(own_blocks, BLK, steps), node_geometry, taps, boundary, sends, cols)


def solution(mesh):
    return jax.shard_map(
        on_device,
        mesh=mesh,
        in_specs=(
            P(("parts", "node", "tm"), None),
            P(None, ("node", "tm")),
            P(),
            P("node", None),
            P(),
            P("node", None),
        ),
        out_specs=P(("parts", "node"), "tm"),
        check_vma=False,
    )
```
